512 devices in a mesh: sector: 32 (over z_hi, x, core), dof: 16 (over z_lo, y).
Axes of the slice: x: 4, y: 8, z: 8 (z_hi: 4, z_lo: 2; z = z_hi * 2 + z_lo), core: 2. Of those that a mesh axis runs over, the one named last changes fastest.
Arguments:
- rhs: float32 [32, 4096, 128], P('sector', 'dof')
- diagonal: float32 [32, 4096], P('sector', 'dof'), may hold values from 4 to 8
- coupling: bfloat16 [32, 4096, 2048], P('sector', 'dof'), may hold values from -0.125 to 0.125
- springs: float32 [32, 3072], P('sector', 'dof'), may hold values from 1 to 4
- precond: bfloat16 [4096, 4096], P('dof')
- hub_inverse: bfloat16 [3072, 3072], P('dof')
Outputs:
- solution: float32 [32, 4096, 128], P('sector', 'dof')
- residual: float32 [32, 4096, 128], P('sector', 'dof')
The draws below stay inside these ranges and needn't reach their ends.
All inputs are finite; a program needn't handle non-finite values.
Results may differ from the reference program's by a relative error of at most 0.0056.
Values may be sent and summed in bfloat16 or wider, within the bound.
A program may use at most 64 MiB of HBM per device.

```python
import math
import jax
import jax.numpy as jnp
from jax import lax

B = 4096
R = 128
ITERS = 3
SECTORS = 32
HUB = 3072
N_DOF = 16


def draw_rhs(key, part):
    first, second = jax.random.split(jax.random.fold_in(key, 11), 2)
    shared = jax.random.normal(first, (B, R), jnp.float32)
    own = jax.random.normal(second, (SECTORS, B, R), jnp.float32)
    return 0.7 * shared[None] + 0.7 * own


def dominant(key, order, scale):
    first, second = jax.random.split(key)
    spread = jax.random.normal(first, (order, order), jnp.float32)
    lead = 1.0 + 0.5 * jax.random.uniform(second, (order,), jnp.float32)
    return scale * (jnp.eye(order, dtype=jnp.float32) * lead[None, :] + 0.3 * spread / order ** 0.5)


def draw_precond(key, part):
    return dominant(jax.random.fold_in(key, 23), B, 1.0 / 6.0).astype(jnp.bfloat16)


def draw_hub_inverse(key, part):
    return dominant(jax.random.fold_in(key, 37), HUB, 1.0 / SECTORS).astype(jnp.bfloat16)


def steps_of(stream_key, extent, shards, least, top_value):
    factor_of = 1.0
    for axis_at, blocks in shards:
        steps = jax.random.uniform(jax.random.fold_in(jax.random.fold_in(stream_key, 6), axis_at), (blocks,), jnp.float32, least / len(shards), top_value / len(shards))
        factor_of = factor_of * jnp.repeat(jnp.exp(steps), extent[axis_at] // blocks).reshape((-1,) + (1,) * (len(extent) - 1 - axis_at))
    return factor_of


def noise(stream_key, shape, width, bound, cuts=(), held_as=jnp.bfloat16):
    array = width * jax.random.normal(stream_key, shape, jnp.float32)
    if cuts:
        array = array * steps_of(stream_key, shape, cuts, -0.22, 0.18)
    return jnp.clip(array, -bound, bound).astype(held_as)


def setup_inputs(seed: int = 0) -> dict:
    streams_of = jax.random.split(jax.random.key(seed), 7)
    return {
        "rhs": draw_rhs(jax.random.fold_in(streams_of[6], 71), 0),
        "diagonal": jnp.clip(4.0 + 4.0 * jax.random.uniform(streams_of[1], (SECTORS, B), jnp.float32) ** steps_of(streams_of[1], (SECTORS, B), ((0, 32), (1, 16)), -0.2, 0.2), 4.0, 8.0),
        "coupling": noise(streams_of[2], (SECTORS, B, B // 2), (B // 2) ** -0.5, 0.125, ((0, 32), (1, 16))),
        "springs": jnp.clip(jnp.exp(math.log(4.0) - 1.3862944 * jax.random.uniform(streams_of[3], (SECTORS, HUB), jnp.float32) ** steps_of(streams_of[3], (SECTORS, HUB), ((0, 32), (1, 16)), -0.2, 0.2)), 1.0, 4.0),
        "precond": draw_precond(jax.random.fold_in(streams_of[6], 71), 0),
        "hub_inverse": draw_hub_inverse(jax.random.fold_in(streams_of[6], 71), 0),
    }


def reference(rhs, diagonal, coupling, springs, precond, hub_inverse):
    rows_dev = B // N_DOF
    quarter = rows_dev // 4

    def apply_pre(field):
        field_low = field.astype(jnp.bfloat16)
        return lax.map(lambda block: jnp.dot(precond, block, preferred_element_type=jnp.float32), field_low)

    def apply_op(field):
        split = field.reshape(SECTORS, N_DOF, rows_dev, R)
        split_low = split.astype(jnp.bfloat16)
        prev_right = jnp.roll(split_low[:, :, quarter:2 * quarter], 1, axis=0)
        next_left = jnp.roll(split_low[:, :, :quarter], -1, axis=0)
        inter = jnp.concatenate([prev_right, next_left], axis=2).reshape(SECTORS, B // 2, R)
        couple = lax.map(lambda pair: jnp.dot(pair[0], pair[1], preferred_element_type=jnp.float32), (coupling, inter))
        spring_rows = springs.reshape(SECTORS, N_DOF, 3 * quarter)[..., None]
        attached = split[:, :, :3 * quarter]
        load = jnp.sum(spring_rows * attached, axis=0).reshape(HUB, R).astype(jnp.bfloat16)
        hub = jnp.dot(hub_inverse, load, preferred_element_type=jnp.float32).reshape(N_DOF, 3 * quarter, R)
        hub_term = spring_rows * (attached - hub[None])
        hub_term = jnp.concatenate([hub_term, jnp.zeros((SECTORS, N_DOF, quarter, R), jnp.float32)], axis=2)
        return diagonal[..., None] * field + couple + hub_term.reshape(SECTORS, B, R)

    solution = jnp.zeros_like(rhs)
    residual = rhs
    for step in range(ITERS):
        precon = apply_pre(residual)
        image = apply_op(precon)
        upper = jnp.sum(image * residual, axis=(0, 1))
        lower = jnp.sum(image * image, axis=(0, 1))
        alpha = upper / (lower + 1e-6)
        solution = solution + alpha * precon
        residual = residual - alpha * image
    return solution, residual
```

```python
import jax
import jax.numpy as jnp
from jax import lax
from jax.experimental import pallas as pl
from jax.experimental.pallas import tpu as pltpu
from jax.sharding import PartitionSpec as P

ITERS = 3
NY, NZL, NZH, NG = 8, 2, 4, 8
PARTS = NY * NZL
QUARTER = 64
ROWS = 4 * QUARTER
FACE = 2 * QUARTER
ATT = 3 * QUARTER
PIECE = ATT // NG
LOADS = 128
MESH = pl.DeviceIdType.MESH

OWN_SENDS = (("r", 0), ("l", 1), ("z", 2))
EVENTS = (
    (0, -1, (("r", 3), ("z", 5))),
    (0, 1, (("l", 4), ("z", 6))),
    (1, 0, ()),
    (0, -2, (("r", 7), ("z", 9))),
    (0, 2, (("l", 8), ("z", 10))),
    (1, -1, ()),
    (1, 1, ()),
    (0, -3, (("r", 11),)),
    (0, 3, ()),
    (1, -2, (("r", 12),)),
    (1, 2, (("l", 13),)),
    (0, -4, ()),
    (1, -3, ()),
    (1, 3, (("l", 14),)),
    (1, 4, ()),
)


def kernel(
    rhs_ref, diag_ref, spring_ref, couple_hbm, pre_hbm, hub_hbm, sol_ref, res_ref,
    pre, coup, hubraw, hubblk, rbuf, fbuf, lbuf, stage, v, acc, cacc, hacc, main, spr,
    part, rs_recv, zsrc, zrecv, asrc, agbuf, dsrc, drecv,
    load_sem, r_send, r_recv, f_send, f_recv, l_send, l_recv, x_send, x_recv,
    rs_send, rs_sem, z_send, z_sem, a_send, a_sem, d_send, d_sem,
):
    s = lax.axis_index("sector")
    d = lax.axis_index("dof")
    zh, g = s // NG, s % NG
    zl, y = d // NY, d % NY
    z = zh * NZL + zl
    nsec = NZH * NG

    def dof_at(column, offset):
        col = zl if column == 0 else 1 - zl
        return col * NY + (y + offset + NY) % NY

    link_dev = {
        "r": (s, dof_at(0, 1)),
        "l": (s, dof_at(0, -1)),
        "z": (s, dof_at(1, 0)),
    }
    y_peer = [(s, zl * NY + (y + j) % NY) for j in range(NY)]
    z_all = [(z + j) % (NZH * NZL) for j in range(NZH * NZL)]
    z_peer = [((zz // NZL) * NG + g, (zz % NZL) * NY + y) for zz in z_all]
    g_index = [(g + j) % NG for j in range(NG)]
    g_peer = [(zh * NG + gg, d) for gg in g_index]
    zh_peer = [(((zh + k) % NZH) * NG + g, d) for k in range(NZH)]
    next_sec = ((s + 1) % nsec, d)
    prev_sec = ((s + nsec - 1) % nsec, d)

    def send(src, dst, ssem, rsem, dev):
        pltpu.make_async_remote_copy(
            src_ref=src, dst_ref=dst, send_sem=ssem, recv_sem=rsem,
            device_id=dev, device_id_type=MESH,
        ).start()

    def arrived(ref, sem):
        pltpu.make_async_copy(ref, ref, sem).wait()

    loads_in = [
        pltpu.make_async_copy(pre_hbm, pre, load_sem.at[0]),
        pltpu.make_async_copy(hub_hbm, hubraw, load_sem.at[1]),
        pltpu.make_async_copy(couple_hbm.at[0], coup, load_sem.at[2]),
    ]
    for c in loads_in:
        c.start()

    barrier = pltpu.get_barrier_semaphore()
    greet = y_peer[1:] + z_peer[1:] + g_peer[1:] + [next_sec, prev_sec]
    for dev in greet:
        pl.semaphore_signal(barrier, inc=1, device_id=dev, device_id_type=MESH)

    res_ref[0] = rhs_ref[0]
    rbuf[d] = rhs_ref[0].astype(jnp.bfloat16)
    sol_ref[0] = jnp.zeros((ROWS, LOADS), jnp.float32)
    sp = jnp.broadcast_to(spring_ref[...], (LOADS, ATT)).T
    spr[...] = sp
    main[...] = jnp.broadcast_to(diag_ref[...], (LOADS, ROWS)).T
    main[:ATT] = main[:ATT] + sp
    dsrc[...] = jnp.zeros(dsrc.shape, jnp.float32)
    pl.semaphore_wait(barrier, len(greet))

    def begin_gather(buf, ssem, rsem):
        for link, there in OWN_SENDS:
            send(buf.at[d], buf.at[d], ssem, rsem.at[there], link_dev[link])

    def take(buf, ssem, rsem, event):
        column, offset, onward = EVENTS[event]
        idx = dof_at(column, offset)
        arrived(buf.at[idx], rsem.at[event])
        for link, there in onward:
            send(buf.at[idx], buf.at[idx], ssem, rsem.at[there], link_dev[link])
        return idx

    begin_gather(rbuf, r_send, r_recv)

    loads_in[1].wait()
    for j in range(PARTS):
        hubblk[j] = hubraw[:, j * ATT:(j + 1) * ATT]
    loads_in[0].wait()
    loads_in[2].wait()

    def pre_dot(idx):
        off = pl.multiple_of(idx * ROWS, ROWS)
        return jnp.dot(pre[:, pl.ds(off, ROWS)], rbuf[idx], preferred_element_type=jnp.float32)

    def couple_dot(idx):
        off = pl.multiple_of(idx * FACE, FACE)
        return jnp.dot(coup[:, pl.ds(off, FACE)], fbuf[idx], preferred_element_type=jnp.float32)

    def hub_dot(idx):
        return jnp.dot(hubblk[idx], lbuf[idx], preferred_element_type=jnp.float32)

    def step(it, carry):
        acc[...] = pre_dot(d)
        for e in range(len(EVENTS)):
            idx = take(rbuf, r_send, r_recv, e)
            acc[...] += pre_dot(idx)
        v[...] = acc[...]
        part[...] = (spr[...] * v[:ATT]).reshape(NG, PIECE, LOADS)
        for j in range(1, NG):
            send(part.at[g_index[j]], rs_recv.at[j], rs_send, rs_sem.at[j], g_peer[j])
        stage[...] = v[:FACE].astype(jnp.bfloat16)
        send(stage.at[pl.ds(QUARTER, QUARTER)], fbuf.at[d, pl.ds(0, QUARTER)], x_send, x_recv.at[0], next_sec)
        send(stage.at[pl.ds(0, QUARTER)], fbuf.at[d, pl.ds(QUARTER, QUARTER)], x_send, x_recv.at[1], prev_sec)
        total = part[g]
        for j in range(1, NG):
            arrived(rs_recv.at[j], rs_sem.at[j])
            total = total + rs_recv[j]
        zsrc[...] = total
        for k in range(1, NZH):
            send(zsrc, zrecv.at[k], z_send, z_sem.at[k], zh_peer[k])
        arrived(fbuf.at[d, pl.ds(0, QUARTER)], x_recv.at[0])
        arrived(fbuf.at[d, pl.ds(QUARTER, QUARTER)], x_recv.at[1])
        begin_gather(fbuf, f_send, f_recv)
        cacc[...] = couple_dot(d)

        def face(e):
            idx = take(fbuf, f_send, f_recv, e)
            cacc[...] += couple_dot(idx)

        def load(e):
            idx = take(lbuf, l_send, l_recv, e)
            hacc[...] += hub_dot(idx)

        for k in range(1, NZH):
            arrived(zrecv.at[k], z_sem.at[k])
            total = total + zrecv[k]
        asrc[...] = total
        for j in range(1, NG):
            send(asrc, agbuf.at[g], a_send, a_sem.at[j], g_peer[j])
        agbuf[g] = total
        for e in range(0, 3):
            face(e)
        for j in range(1, NG):
            arrived(agbuf.at[(g + NG - j) % NG], a_sem.at[j])
        lbuf[d] = agbuf[...].reshape(ATT, LOADS).astype(jnp.bfloat16)
        begin_gather(lbuf, l_send, l_recv)
        hacc[...] = hub_dot(d)
        for e in range(3, 7):
            face(e)
        for e in range(0, 3):
            load(e)
        for e in range(7, 11):
            face(e)
        for e in range(3, 7):
            load(e)
        for e in range(11, 15):
            face(e)
        for e in range(7, 15):
            load(e)

        acc[...] = main[...] * v[...] + cacc[...]
        acc[:ATT] = acc[:ATT] - spr[...] * hacc[...]
        arrived(rbuf.at[pl.ds(0, 15)], r_send)
        arrived(fbuf.at[pl.ds(0, 15)], f_send)
        arrived(lbuf.at[pl.ds(0, 15)], l_send)
        arrived(stage, x_send)
        arrived(part.at[pl.ds(0, NG - 1)], rs_send)
        arrived(part.at[pl.ds(0, NZH - 1)], z_send)
        arrived(part.at[pl.ds(0, NG - 1)], a_send)
        image = acc[...]
        up = jnp.sum(image * res_ref[0], axis=0, keepdims=True)
        low = jnp.sum(image * image, axis=0, keepdims=True)
        dsrc[0, 0:1] = up
        dsrc[0, 1:2] = low
        for p, peers in enumerate((y_peer, z_peer, g_peer)):
            for j in range(1, 8):
                send(dsrc.at[p], drecv.at[p, j], d_send.at[p], d_sem.at[p, j], peers[j])
            total = dsrc[p]
            for j in range(1, 8):
                arrived(drecv.at[p, j], d_sem.at[p, j])
                total = total + drecv[p, j]
            dsrc[p + 1] = total
        alpha = dsrc[3, 0:1] / (dsrc[3, 1:2] + 1e-06)
        res = res_ref[0] - alpha * acc[...]
        for p in range(3):
            arrived(drecv.at[p, pl.ds(0, 7)], d_send.at[p])

        @pl.when(it < ITERS - 1)
        def _():
            rbuf[d] = res.astype(jnp.bfloat16)
            begin_gather(rbuf, r_send, r_recv)

        res_ref[0] = res
        sol_ref[0] = sol_ref[0] + alpha * v[...]
        return carry

    lax.fori_loop(0, ITERS, step, 0)


def body(rhs, diagonal, coupling, springs, precond, hub_inverse):
    vm = pl.BlockSpec(memory_space=pltpu.VMEM)
    hbm = pl.BlockSpec(memory_space=pl.ANY)
    f32, bf16 = jnp.float32, jnp.bfloat16
    dma = pltpu.SemaphoreType.DMA
    n = len(EVENTS)
    return pl.pallas_call(
        kernel,
        out_shape=(
            jax.ShapeDtypeStruct((1, ROWS, LOADS), f32),
            jax.ShapeDtypeStruct((1, ROWS, LOADS), f32),
        ),
        in_specs=[vm, vm, vm, hbm, hbm, hbm],
        out_specs=(vm, vm),
        scratch_shapes=[
            pltpu.VMEM((ROWS, PARTS * ROWS), bf16),
            pltpu.VMEM((ROWS, PARTS * FACE), bf16),
            pltpu.VMEM((ATT, PARTS * ATT), bf16),
            pltpu.VMEM((PARTS, ATT, ATT), bf16),
            pltpu.VMEM((PARTS, ROWS, LOADS), bf16),
            pltpu.VMEM((PARTS, FACE, LOADS), bf16),
            pltpu.VMEM((PARTS, ATT, LOADS), bf16),
            pltpu.VMEM((FACE, LOADS), bf16),
            pltpu.VMEM((ROWS, LOADS), f32),
            pltpu.VMEM((ROWS, LOADS), f32),
            pltpu.VMEM((ROWS, LOADS), f32),
            pltpu.VMEM((ATT, LOADS), f32),
            pltpu.VMEM((ROWS, LOADS), f32),
            pltpu.VMEM((ATT, LOADS), f32),
            pltpu.VMEM((NG, PIECE, LOADS), f32),
            pltpu.VMEM((NG, PIECE, LOADS), f32),
            pltpu.VMEM((PIECE, LOADS), f32),
            pltpu.VMEM((NZH, PIECE, LOADS), f32),
            pltpu.VMEM((PIECE, LOADS), f32),
            pltpu.VMEM((NG, PIECE, LOADS), f32),
            pltpu.VMEM((4, 8, LOADS), f32),
            pltpu.VMEM((3, 8, 8, LOADS), f32),
            dma((3,)),
            dma, dma((n,)),
            dma, dma((n,)),
            dma, dma((n,)),
            dma, dma((2,)),
            dma, dma((NG,)),
            dma, dma((NZH,)),
            dma, dma((NG,)),
            dma((3,)), dma((3, 8)),
        ],
        compiler_params=pltpu.CompilerParams(
            collective_id=0, has_side_effects=True, vmem_limit_bytes=40 * 1024 * 1024
        ),
    )(rhs, diagonal, springs, coupling, precond, hub_inverse)


def solution(mesh):
    placed = (
        P("sector", "dof", None),
        P("sector", "dof"),
        P("sector", "dof", None),
        P("sector", "dof"),
        P("dof", None),
        P("dof", None),
    )
    return jax.shard_map(
        body,
        mesh=mesh,
        in_specs=placed,
        out_specs=(P("sector", "dof", None), P("sector", "dof", None)),
        check_vma=False,
    )
```

```python
import jax
import jax.numpy as jnp
from jax import lax
from jax.experimental import pallas as pl
from jax.experimental.pallas import tpu as pltpu
from jax.sharding import PartitionSpec as P

ITERS = 3
NX, NY, NZL, NZH = 4, 8, 2, 4
NZ = NZL * NZH
PARTS = NY * NZL
QUARTER = 64
ROWS = 4 * QUARTER
FACE = 2 * QUARTER
ATT = 3 * QUARTER
HALF = ATT // 2
LOADS = 128
MESH = pl.DeviceIdType.MESH

NEAR = (-1, 1, -2, 2, -3, 3, 4)
COLUMN = len(NEAR)
BLOCKS = 2 * COLUMN + 1


def kernel(
    rhs_ref, diag_ref, spring_ref, couple_hbm, pre_hbm, hub_hbm, sol_ref, res_ref,
    pre, coup, hubraw, hubblk, rbuf, fbuf, lbuf, qold, qnew, stage, v, acc, cacc, hacc, hrecv,
    main, spr, csend, crecv, xsend, xrecv, zsend, zrecv, dsrc, dof_dots, pair_src, pair_dots, all_dots,
    load_sem, r_send, r_sem, f_send, f_sem, n_send, n_sem, c_send, c_sem, x_send, x_sem,
    z_send, z_sem, y_send, y_sem, h_send, h_sem, d_send, d_sem, p_send, p_sem, a_send, a_sem,
):
    s = lax.axis_index("sector")
    d = lax.axis_index("dof")
    zh, x, c = s // (2 * NX), (s // 2) % NX, s % 2
    zl, y = d // NY, d % NY
    z = zh * NZL + zl
    plane = zh * NX + x
    nsec = NZH * NX * 2

    def sector_of(zh, x, c):
        return (zh * NX + x) * 2 + c

    def dof_at(column, offset):
        col = zl if column == 0 else 1 - zl
        return col * NY + (y + offset + NY) % NY

    y_peer = [(s, zl * NY + (y + j) % NY) for j in range(NY)]
    z_at = [(z + j) % NZ for j in range(NZ)]
    z_peer = [(sector_of(zz // NZL, x, c), (zz % NZL) * NY + y) for zz in z_at]
    x_peer = [(sector_of(zh, (x + j) % NX, c), d) for j in range(NX)]
    dof_peer = [(s, (d + j) % PARTS) for j in range(PARTS)]
    plane_at = [(plane + j) % (NZH * NX) for j in range(NZH * NX)]
    plane_peer = [(m * 2 + c, d) for m in plane_at]
    partner = (s, dof_at(1, 0))
    sibling = (sector_of(zh, x, 1 - c), d)
    next_sec = ((s + 1) % nsec, d)
    prev_sec = ((s + nsec - 1) % nsec, d)

    def send(src, dst, ssem, rsem, dev):
        pltpu.make_async_remote_copy(
            src_ref=src, dst_ref=dst, send_sem=ssem, recv_sem=rsem,
            device_id=dev, device_id_type=MESH,
        ).start()

    def arrived(ref, sem):
        pltpu.make_async_copy(ref, ref, sem).wait()

    loads_in = [
        pltpu.make_async_copy(pre_hbm, pre, load_sem.at[0]),
        pltpu.make_async_copy(hub_hbm, hubraw, load_sem.at[1]),
        pltpu.make_async_copy(couple_hbm.at[0], coup, load_sem.at[2]),
    ]
    for copy in loads_in:
        copy.start()

    barrier = pltpu.get_barrier_semaphore()
    greet = dof_peer[1:] + plane_peer[1:] + z_peer[1::2] + [sibling, next_sec, prev_sec]
    for dev in greet:
        pl.semaphore_signal(barrier, inc=1, device_id=dev, device_id_type=MESH)

    res_ref[0] = rhs_ref[0]
    rbuf[d] = rhs_ref[0].astype(jnp.bfloat16)
    sol_ref[0] = jnp.zeros((ROWS, LOADS), jnp.float32)
    sp = jnp.broadcast_to(spring_ref[...], (LOADS, ATT)).T
    spr[...] = sp
    main[...] = jnp.broadcast_to(diag_ref[...], (LOADS, ROWS)).T
    main[:ATT] = main[:ATT] + sp
    dsrc[...] = jnp.zeros(dsrc.shape, jnp.float32)
    pl.semaphore_wait(barrier, len(greet))

    def begin_gather(buf, ssem, rsem):
        for k, offset in enumerate(NEAR):
            send(buf.at[d], buf.at[d], ssem, rsem.at[k], (s, dof_at(0, -offset)))
        send(buf.at[d], buf.at[d], ssem, rsem.at[COLUMN], partner)

    def take(buf, ssem, rsem, event):
        if event < COLUMN:
            idx = dof_at(0, NEAR[event])
        elif event == COLUMN:
            idx = dof_at(1, 0)
        else:
            idx = dof_at(1, NEAR[event - COLUMN - 1])
        arrived(buf.at[idx], rsem.at[event])
        if event < COLUMN:
            send(buf.at[idx], buf.at[idx], ssem, rsem.at[COLUMN + 1 + event], partner)
        return idx

    def pre_dot(idx):
        off = pl.multiple_of(idx * ROWS, ROWS)
        return jnp.dot(pre[:, pl.ds(off, ROWS)], rbuf[idx], preferred_element_type=jnp.float32)

    def couple_dot(idx):
        off = pl.multiple_of(idx * FACE, FACE)
        return jnp.dot(coup[:, pl.ds(off, FACE)], fbuf[idx], preferred_element_type=jnp.float32)

    def hub_dot(idx):
        rows = lbuf[idx].reshape(ATT, LOADS)
        return jnp.dot(hubblk[idx], rows, preferred_element_type=jnp.float32)

    def ratio(squares, low):
        return jnp.clip(jnp.sqrt(squares / jnp.maximum(low, 1e-30)), 1e-12, 1e12)

    def image_of_v():
        other = pl.multiple_of((1 - c) * HALF, 8)
        mine = pl.multiple_of(c * HALF, 8)
        csend[...] = spr[pl.ds(other, HALF)] * v[pl.ds(other, HALF)]
        send(csend, crecv, c_send, c_sem, sibling)
        stage[...] = v[:FACE].astype(jnp.bfloat16)
        right, left = pl.ds(QUARTER, QUARTER), pl.ds(0, QUARTER)
        send(stage.at[right], fbuf.at[d, left], n_send, n_sem.at[0], next_sec)
        send(stage.at[left], fbuf.at[d, right], n_send, n_sem.at[1], prev_sec)
        part = spr[pl.ds(mine, HALF)] * v[pl.ds(mine, HALF)]
        arrived(crecv, c_sem)
        part = part + crecv[...]
        xsend[...] = part
        for j in range(1, NX):
            send(xsend, xrecv.at[j], x_send, x_sem.at[j], x_peer[j])
        arrived(fbuf.at[d, left], n_sem.at[0])
        arrived(fbuf.at[d, right], n_sem.at[1])
        begin_gather(fbuf, f_send, f_sem)
        for j in range(1, NX):
            arrived(xrecv.at[j], x_sem.at[j])
            part = part + xrecv[j]
        zsend[...] = part.astype(jnp.bfloat16)
        for j in range(1, NZ):
            send(zsend, zrecv.at[j], z_send, z_sem.at[j], z_peer[j])
        cacc[...] = couple_dot(d)

        def face(event):
            cacc[...] += couple_dot(take(fbuf, f_send, f_sem, event))

        for event in range(COLUMN):
            face(event)
        across = jnp.zeros((HALF, LOADS), jnp.float32)
        for j in range(1, NZ):
            arrived(zrecv.at[j], z_sem.at[j])
            term = zrecv[j].astype(jnp.float32)
            if j % 2 == 0:
                part = part + term
            else:
                across = across + term
        lbuf[y, zl] = part.astype(jnp.bfloat16)
        lbuf[y, 1 - zl] = across.astype(jnp.bfloat16)
        for j in range(1, NY):
            send(lbuf.at[y], lbuf.at[y], y_send, y_sem.at[j], y_peer[j])
        hacc[...] = hub_dot(y)
        for event in range(COLUMN, BLOCKS):
            face(event)
        acc[...] = main[...] * v[...] + cacc[...]
        for j in range(1, NY):
            idx = (y + NY - j) % NY
            arrived(lbuf.at[idx], y_sem.at[j])
            hacc[...] += hub_dot(idx)
        send(hacc, hrecv, h_send, h_sem, sibling)
        arrived(csend, c_send)
        arrived(stage, n_send)
        arrived(xrecv.at[pl.ds(0, NX - 1)], x_send)
        arrived(fbuf.at[pl.ds(0, BLOCKS)], f_send)
        arrived(zrecv.at[pl.ds(0, NZ - 1)], z_send)
        arrived(lbuf.at[pl.ds(0, NY - 1)], y_send)
        arrived(hrecv, h_sem)
        acc[:ATT] = acc[:ATT] - spr[...] * (hacc[...] + hrecv[...])
        arrived(hacc, h_send)

    def column_sum(a):
        return jnp.sum(a, axis=0, keepdims=True)

    def dots_begin():
        for j in range(1, PARTS):
            send(dsrc, dof_dots.at[d], d_send, d_sem.at[j], dof_peer[j])
        dof_dots[d] = dsrc[...]

    def dots_pair():
        for j in range(1, PARTS):
            arrived(dof_dots.at[(d + PARTS - j) % PARTS], d_sem.at[j])
        pair_src[...] = jnp.sum(dof_dots[...], axis=0)
        send(pair_src, pair_dots, p_send, p_sem, sibling)

    def dots_plane():
        arrived(pair_dots, p_sem)
        all_dots[plane] = pair_src[...] + pair_dots[...]
        for j in range(1, NZH * NX):
            send(all_dots.at[plane], all_dots.at[plane], a_send, a_sem.at[j], plane_peer[j])

    def dots_end():
        for j in range(1, NZH * NX):
            arrived(all_dots.at[(plane + NZH * NX - j) % (NZH * NX)], a_sem.at[j])
        total = jnp.sum(all_dots[...], axis=0)
        arrived(dof_dots.at[pl.ds(0, PARTS - 1)], d_send)
        arrived(pair_src, p_send)
        arrived(all_dots.at[pl.ds(0, NZH * NX - 1)], a_send)
        return total[0:1] / (total[1:2] + 1e-06)

    def local_dots():
        image, res = acc[...], res_ref[0]
        low, squares = column_sum(image * image), column_sum(res * res)
        dsrc[0:1] = column_sum(image * res)
        dsrc[1:2] = low
        dsrc[2:3] = squares
        return ratio(squares, low)

    def advance(alpha):
        sol_ref[0] = sol_ref[0] + alpha * v[...]
        res_ref[0] = res_ref[0] - alpha * acc[...]

    begin_gather(rbuf, r_send, r_sem)
    loads_in[1].wait()
    for core in range(2):
        @pl.when(c == core)
        def _():
            for k in range(NY):
                for col in range(NZL):
                    at = (col * NY + k) * ATT + core * HALF
                    hubblk[k, :, col * HALF:(col + 1) * HALF] = hubraw[:, at:at + HALF]
    loads_in[0].wait()
    loads_in[2].wait()
    qold[d] = pre_dot(d)
    for event in range(BLOCKS):
        idx = take(rbuf, r_send, r_sem, event)
        qold[idx] = pre_dot(idx)
    total = qold[0]
    for k in range(1, PARTS):
        total = total + qold[k]
    v[...] = total
    arrived(rbuf.at[pl.ds(0, BLOCKS)], r_send)

    def step(it, carry):
        image_of_v()
        trial = local_dots()
        rbuf[d] = (res_ref[0] - trial * acc[...]).astype(jnp.bfloat16)
        begin_gather(rbuf, r_send, r_sem)
        dots_begin()
        qnew[d] = pre_dot(d)

        def block(event):
            idx = take(rbuf, r_send, r_sem, event)
            qnew[idx] = pre_dot(idx)

        for event in range(COLUMN):
            block(event)
        dots_pair()
        block(COLUMN)
        block(COLUMN + 1)
        dots_plane()
        for event in range(COLUMN + 2, BLOCKS):
            block(event)
        alpha = dots_end()
        arrived(rbuf.at[pl.ds(0, BLOCKS)], r_send)
        advance(alpha)
        total = jnp.zeros((ROWS, LOADS), jnp.float32)
        for k in range(PARTS):
            grow = alpha / ratio(dof_dots[k, 2:3], dof_dots[k, 1:2])
            q = grow * qnew[k] - (grow - 1.0) * qold[k]
            qold[k] = q
            total = total + q
        v[...] = total
        return carry

    lax.fori_loop(0, ITERS - 1, step, 0)
    image_of_v()
    local_dots()
    dots_begin()
    dots_pair()
    dots_plane()
    advance(dots_end())


def body(rhs, diagonal, coupling, springs, precond, hub_inverse):
    vm = pl.BlockSpec(memory_space=pltpu.VMEM)
    hbm = pl.BlockSpec(memory_space=pl.ANY)
    f32, bf16 = jnp.float32, jnp.bfloat16
    dma = pltpu.SemaphoreType.DMA
    mem = pltpu.VMEM
    return pl.pallas_call(
        kernel,
        out_shape=(
            jax.ShapeDtypeStruct((1, ROWS, LOADS), f32),
            jax.ShapeDtypeStruct((1, ROWS, LOADS), f32),
        ),
        in_specs=[vm, vm, vm, hbm, hbm, hbm],
        out_specs=(vm, vm),
        scratch_shapes=[
            mem((ROWS, PARTS * ROWS), bf16),
            mem((ROWS, PARTS * FACE), bf16),
            mem((ATT, PARTS * ATT), bf16),
            mem((NY, ATT, ATT), bf16),
            mem((PARTS, ROWS, LOADS), bf16),
            mem((PARTS, FACE, LOADS), bf16),
            mem((NY, NZL, HALF, LOADS), bf16),
            mem((PARTS, ROWS, LOADS), f32),
            mem((PARTS, ROWS, LOADS), f32),
            mem((FACE, LOADS), bf16),
            mem((ROWS, LOADS), f32),
            mem((ROWS, LOADS), f32),
            mem((ROWS, LOADS), f32),
            mem((ATT, LOADS), f32),
            mem((ATT, LOADS), f32),
            mem((ROWS, LOADS), f32),
            mem((ATT, LOADS), f32),
            mem((HALF, LOADS), f32),
            mem((HALF, LOADS), f32),
            mem((HALF, LOADS), f32),
            mem((NX, HALF, LOADS), f32),
            mem((HALF, LOADS), bf16),
            mem((NZ, HALF, LOADS), bf16),
            mem((8, LOADS), f32),
            mem((PARTS, 8, LOADS), f32),
            mem((8, LOADS), f32),
            mem((8, LOADS), f32),
            mem((NZH * NX, 8, LOADS), f32),
            dma((3,)),
            dma, dma((BLOCKS,)),
            dma, dma((BLOCKS,)),
            dma, dma((2,)),
            dma, dma,
            dma, dma((NX,)),
            dma, dma((NZ,)),
            dma, dma((NY,)),
            dma, dma,
            dma, dma((PARTS,)),
            dma, dma,
            dma, dma((NZH * NX,)),
        ],
        compiler_params=pltpu.CompilerParams(
            collective_id=0, has_side_effects=True, vmem_limit_bytes=40 * 1024 * 1024
        ),
    )(rhs, diagonal, springs, coupling, precond, hub_inverse)


def solution(mesh):
    placed = (
        P("sector", "dof", None),
        P("sector", "dof"),
        P("sector", "dof", None),
        P("sector", "dof"),
        P("dof", None),
        P("dof", None),
    )
    return jax.shard_map(
        body,
        mesh=mesh,
        in_specs=placed,
        out_specs=(P("sector", "dof", None), P("sector", "dof", None)),
        check_vma=False,
    )
```

```python
import jax
import jax.numpy as jnp
from jax import lax
from jax.experimental import pallas as pl
from jax.experimental.pallas import tpu as pltpu
from jax.sharding import PartitionSpec as P

ITERS = 3
NX, NY, NZL, NZH = 4, 8, 2, 4
NZ = NZL * NZH
PARTS = NY * NZL
QUARTER = 64
ROWS = 4 * QUARTER
FACE = 2 * QUARTER
ATT = 3 * QUARTER
HALF = ATT // 2
LOADS = 128
MESH = pl.DeviceIdType.MESH

NEAR = (-1, 1, -2, 2, -3, 3, 4)
COLUMN = len(NEAR)
BLOCKS = 2 * COLUMN + 1


def kernel(
    rhs_hbm, diag_hbm, spring_hbm, couple_hbm, pre_hbm, hub_hbm, sol_ref, res_ref,
    diag_row, spring_row, pre, coup, hubraw, hubblk, rbuf, fbuf, lbuf, qold, qnew, stage,
    v, vec, image, acc, cacc, hacc, hrecv, main, spr, csend, crecv, xsend, xrecv, zsend, zrecv, dsrc, dof_dots, pair_src, pair_dots, all_dots,
    load_sem, r_send, r_sem, f_send, f_sem, n_send, n_sem, c_send, c_sem, x_send, x_sem,
    z_send, z_sem, y_send, y_sem, h_send, h_sem, d_send, d_sem, p_send, p_sem, a_send, a_sem,
):
    s = lax.axis_index("sector")
    d = lax.axis_index("dof")
    zh, x, c = s // (2 * NX), (s // 2) % NX, s % 2
    zl, y = d // NY, d % NY
    z = zh * NZL + zl
    plane = zh * NX + x
    nsec = NZH * NX * 2

    def sector_of(zh, x, c):
        return (zh * NX + x) * 2 + c

    def dof_at(column, offset):
        col = zl if column == 0 else 1 - zl
        return col * NY + (y + offset + NY) % NY

    y_peer = [(s, zl * NY + (y + j) % NY) for j in range(NY)]
    z_at = [(z + j) % NZ for j in range(NZ)]
    z_peer = [(sector_of(zz // NZL, x, c), (zz % NZL) * NY + y) for zz in z_at]
    x_peer = [(sector_of(zh, (x + j) % NX, c), d) for j in range(NX)]
    dof_peer = [(s, (d + j) % PARTS) for j in range(PARTS)]
    plane_at = [(plane + j) % (NZH * NX) for j in range(NZH * NX)]
    plane_peer = [(m * 2 + c, d) for m in plane_at]
    partner = (s, dof_at(1, 0))
    sibling = (sector_of(zh, x, 1 - c), d)
    next_sec = ((s + 1) % nsec, d)
    prev_sec = ((s + nsec - 1) % nsec, d)

    def send(src, dst, ssem, rsem, dev):
        pltpu.make_async_remote_copy(
            src_ref=src, dst_ref=dst, send_sem=ssem, recv_sem=rsem,
            device_id=dev, device_id_type=MESH,
        ).start()

    def arrived(ref, sem):
        pltpu.make_async_copy(ref, ref, sem).wait()

    loads_in = [
        pltpu.make_async_copy(rhs_hbm, res_ref, load_sem.at[0]),
        pltpu.make_async_copy(pre_hbm, pre, load_sem.at[1]),
        pltpu.make_async_copy(diag_hbm, diag_row, load_sem.at[2]),
        pltpu.make_async_copy(spring_hbm, spring_row, load_sem.at[3]),
        pltpu.make_async_copy(hub_hbm, hubraw, load_sem.at[4]),
        pltpu.make_async_copy(couple_hbm.at[0], coup, load_sem.at[5]),
    ]
    for copy in loads_in:
        copy.start()

    barrier = pltpu.get_barrier_semaphore()
    greet = dof_peer[1:] + plane_peer[1:] + z_peer[1::2] + [sibling, next_sec, prev_sec]
    for dev in greet:
        pl.semaphore_signal(barrier, inc=1, device_id=dev, device_id_type=MESH)

    loads_in[0].wait()
    rbuf[d] = res_ref[0].astype(jnp.bfloat16)
    pl.semaphore_wait(barrier, len(greet))

    def begin_gather(buf, ssem, rsem):
        for k, offset in enumerate(NEAR):
            send(buf.at[d], buf.at[d], ssem, rsem.at[k], (s, dof_at(0, -offset)))
        send(buf.at[d], buf.at[d], ssem, rsem.at[COLUMN], partner)

    def take(buf, ssem, rsem, event):
        idx = dof_at(0, NEAR[event])
        arrived(buf.at[idx], rsem.at[event])
        send(buf.at[idx], buf.at[idx], ssem, rsem.at[COLUMN], partner)
        return idx

    across_first = (1 - zl) * NY

    def take_across(buf, rsem):
        arrived(buf.at[pl.ds(across_first, NY)], rsem.at[COLUMN])

    def pre_dot(idx):
        off = pl.multiple_of(idx * ROWS, ROWS)
        return jnp.dot(pre[:, pl.ds(off, ROWS)], rbuf[idx], preferred_element_type=jnp.float32)

    def couple_dot(faces, first, count):
        off = pl.multiple_of(first * FACE, FACE)
        rows = faces[pl.ds(first, count)].reshape(count * FACE, LOADS)
        return jnp.dot(coup[:, pl.ds(off, count * FACE)], rows, preferred_element_type=jnp.float32)

    def ratio(squares, low):
        return jnp.clip(jnp.sqrt(squares / jnp.maximum(low, 1e-30)), 1e-12, 1e12)

    def apply_operator(turn, late):
        faces = fbuf.at[turn]
        other = pl.multiple_of((1 - c) * HALF, 8)
        mine = pl.multiple_of(c * HALF, 8)
        csend[...] = spr[pl.ds(other, HALF)] * vec[pl.ds(other, HALF)]
        send(csend, crecv, c_send, c_sem, sibling)
        stage[...] = vec[:FACE].astype(jnp.bfloat16)
        right, left = pl.ds(QUARTER, QUARTER), pl.ds(0, QUARTER)
        send(stage.at[right], faces.at[d, left], n_send, n_sem.at[turn, 0], next_sec)
        send(stage.at[left], faces.at[d, right], n_send, n_sem.at[turn, 1], prev_sec)
        part = spr[pl.ds(mine, HALF)] * vec[pl.ds(mine, HALF)]
        arrived(crecv, c_sem)
        part = part + crecv[...]
        xsend[...] = part
        for j in range(1, NX):
            send(xsend, xrecv.at[turn, j], x_send, x_sem.at[turn], x_peer[j])
        arrived(faces.at[d, left], n_sem.at[turn, 0])
        arrived(faces.at[d, right], n_sem.at[turn, 1])
        begin_gather(faces, f_send, f_sem)
        arrived(xrecv.at[turn, pl.ds(1, NX - 1)], x_sem.at[turn])
        part = part + xrecv[turn, 1] + xrecv[turn, 2] + xrecv[turn, 3]
        zsend[...] = part.astype(jnp.bfloat16)
        for j in range(1, NZ):
            send(zsend, zrecv.at[turn, j], z_send, z_sem.at[turn], z_peer[j])
        cacc[...] = couple_dot(faces, d, 1)
        for event in range(COLUMN):
            cacc[...] += couple_dot(faces, take(faces, f_send, f_sem, event), 1)
        arrived(zrecv.at[turn, pl.ds(1, NZ - 1)], z_sem.at[turn])
        across = zrecv[turn, 1].astype(jnp.float32)
        for j in range(2, NZ):
            term = zrecv[turn, j].astype(jnp.float32)
            if j % 2 == 0:
                part = part + term
            else:
                across = across + term
        lbuf[y, zl] = part.astype(jnp.bfloat16)
        lbuf[y, 1 - zl] = across.astype(jnp.bfloat16)
        for j in range(1, NY):
            send(lbuf.at[y], lbuf.at[y], y_send, y_sem, y_peer[j])
        take_across(faces, f_sem)
        acc[...] = main[...] * vec[...] + cacc[...] + couple_dot(faces, across_first, NY)
        late()
        arrived(csend, c_send)
        arrived(stage, n_send)
        arrived(xrecv.at[turn, pl.ds(0, NX - 1)], x_send)
        arrived(faces.at[pl.ds(0, BLOCKS)], f_send)
        arrived(zrecv.at[turn, pl.ds(0, NZ - 1)], z_send)
        arrived(lbuf.at[pl.ds(0, NY - 1)], y_send)
        arrived(lbuf.at[pl.ds(0, NY - 1)], y_sem)
        rows = lbuf[...].reshape(NY * ATT, LOADS)
        hacc[...] = jnp.dot(hubblk[...], rows, preferred_element_type=jnp.float32)
        send(hacc, hrecv, h_send, h_sem, sibling)
        arrived(hrecv, h_sem)
        acc[:ATT] = acc[:ATT] - spr[...] * (hacc[...] + hrecv[...])
        arrived(hacc, h_send)

    def column_sum(a):
        return jnp.sum(a, axis=0, keepdims=True)

    def dots_begin():
        for j in range(1, PARTS):
            send(dsrc, dof_dots.at[d], d_send, d_sem, dof_peer[j])
        dof_dots[d] = dsrc[...]

    def dots_pair():
        arrived(dof_dots.at[pl.ds(0, PARTS - 1)], d_sem)
        pair_src[...] = jnp.sum(dof_dots[...], axis=0)
        send(pair_src, pair_dots, p_send, p_sem, sibling)

    def dots_plane(turn):
        arrived(pair_dots, p_sem)
        dots = all_dots.at[turn]
        dots[plane] = pair_src[...] + pair_dots[...]
        for j in range(1, NZH * NX):
            send(dots.at[plane], dots.at[plane], a_send, a_sem.at[turn], plane_peer[j])

    def dots_end(turn):
        arrived(all_dots.at[turn, pl.ds(0, NZH * NX - 1)], a_sem.at[turn])
        total = jnp.sum(all_dots[turn], axis=0)
        arrived(dof_dots.at[pl.ds(0, PARTS - 1)], d_send)
        arrived(pair_src, p_send)
        arrived(all_dots.at[turn, pl.ds(0, NZH * NX - 1)], a_send)
        return total[0:1] / (total[1:2] + 1e-06)

    def local_dots():
        im, res = image[...], res_ref[0]
        low, squares = column_sum(im * im), column_sum(res * res)
        dsrc[0:1] = column_sum(im * res)
        dsrc[1:2] = low
        dsrc[2:3] = squares
        return ratio(squares, low)

    def advance(alpha):
        sol_ref[0] = sol_ref[0] + alpha * v[...]
        res_ref[0] = res_ref[0] - alpha * image[...]

    begin_gather(rbuf, r_send, r_sem)
    for copy in loads_in[1:]:
        copy.wait()
    sp = jnp.broadcast_to(spring_row[...], (LOADS, ATT)).T
    spr[...] = sp
    main[...] = jnp.broadcast_to(diag_row[...], (LOADS, ROWS)).T
    main[:ATT] = main[:ATT] + sp
    sol_ref[0] = jnp.zeros((ROWS, LOADS), jnp.float32)
    dsrc[...] = jnp.zeros(dsrc.shape, jnp.float32)

    def first(idx):
        qold[idx] = pre_dot(idx)

    first(d)
    for event in range(COLUMN):
        first(take(rbuf, r_send, r_sem, event))
    for core in range(2):
        @pl.when(c == core)
        def _():
            for k in range(NY):
                for col in range(NZL):
                    at, to = (col * NY + k) * ATT + core * HALF, k * ATT + col * HALF
                    hubblk[:, to:to + HALF] = hubraw[:, at:at + HALF]
    take_across(rbuf, r_sem)
    for k in range(NY):
        first(across_first + k)
    total = qold[0]
    for k in range(1, PARTS):
        total = total + qold[k]
    vec[...] = total
    v[...] = total
    arrived(rbuf.at[pl.ds(0, BLOCKS)], r_send)
    apply_operator(0, lambda: None)
    image[...] = acc[...]

    def step(it, carry):
        turn = it % 2
        trial = local_dots()
        rbuf[d] = (res_ref[0] - trial * image[...]).astype(jnp.bfloat16)
        begin_gather(rbuf, r_send, r_sem)
        dots_begin()
        qnew[d] = pre_dot(d)
        for event in range(COLUMN):
            idx = take(rbuf, r_send, r_sem, event)
            qnew[idx] = pre_dot(idx)
            if event == 4:
                dots_pair()
        dots_plane(turn)

        def slope(idx, product):
            diff = (product - qold[idx]) / ratio(dof_dots[idx, 2:3], dof_dots[idx, 1:2])
            qnew[idx] = diff
            return diff

        total = jnp.zeros((ROWS, LOADS), jnp.float32)
        for k in range(NY):
            total = total + slope(zl * NY + k, qnew[zl * NY + k])
        take_across(rbuf, r_sem)
        for k in range(NY):
            total = total + slope(across_first + k, pre_dot(across_first + k))
        arrived(rbuf.at[pl.ds(0, BLOCKS)], r_send)
        alpha = dots_end(turn)
        vec[...] = v[...] + alpha * total

        def late():
            advance(alpha)
            v[...] = vec[...]
            for k in range(PARTS):
                qold[k] = qold[k] + alpha * qnew[k]

        apply_operator((it + 1) % 2, late)
        image[...] = acc[...]
        return carry

    lax.fori_loop(0, ITERS - 1, step, 0)
    last = (ITERS - 1) % 2
    local_dots()
    dots_begin()
    dots_pair()
    dots_plane(last)
    advance(dots_end(last))


def body(rhs, diagonal, coupling, springs, precond, hub_inverse):
    vm = pl.BlockSpec(memory_space=pltpu.VMEM)
    hbm = pl.BlockSpec(memory_space=pltpu.HBM)
    f32, bf16 = jnp.float32, jnp.bfloat16
    dma = pltpu.SemaphoreType.DMA
    mem = pltpu.VMEM
    return pl.pallas_call(
        kernel,
        out_shape=(
            jax.ShapeDtypeStruct((1, ROWS, LOADS), f32),
            jax.ShapeDtypeStruct((1, ROWS, LOADS), f32),
        ),
        in_specs=[hbm] * 6,
        out_specs=(vm, vm),
        scratch_shapes=[
            mem((1, ROWS), f32),
            mem((1, ATT), f32),
            mem((ROWS, PARTS * ROWS), bf16),
            mem((ROWS, PARTS * FACE), bf16),
            mem((ATT, PARTS * ATT), bf16),
            mem((ATT, NY * ATT), bf16),
            mem((PARTS, ROWS, LOADS), bf16),
            mem((2, PARTS, FACE, LOADS), bf16),
            mem((NY, NZL, HALF, LOADS), bf16),
            mem((PARTS, ROWS, LOADS), f32),
            mem((PARTS, ROWS, LOADS), f32),
            mem((FACE, LOADS), bf16),
            mem((ROWS, LOADS), f32),
            mem((ROWS, LOADS), f32),
            mem((ROWS, LOADS), f32),
            mem((ROWS, LOADS), f32),
            mem((ROWS, LOADS), f32),
            mem((ATT, LOADS), f32),
            mem((ATT, LOADS), f32),
            mem((ROWS, LOADS), f32),
            mem((ATT, LOADS), f32),
            mem((HALF, LOADS), f32),
            mem((HALF, LOADS), f32),
            mem((HALF, LOADS), f32),
            mem((2, NX, HALF, LOADS), f32),
            mem((HALF, LOADS), bf16),
            mem((2, NZ, HALF, LOADS), bf16),
            mem((8, LOADS), f32),
            mem((PARTS, 8, LOADS), f32),
            mem((8, LOADS), f32),
            mem((8, LOADS), f32),
            mem((2, NZH * NX, 8, LOADS), f32),
            dma((6,)),
            dma, dma((COLUMN + 1,)),
            dma, dma((COLUMN + 1,)),
            dma, dma((2, 2)),
            dma, dma,
            dma, dma((2,)),
            dma, dma((2,)),
            dma, dma,
            dma, dma,
            dma, dma,
            dma, dma,
            dma, dma((2,)),
        ],
        compiler_params=pltpu.CompilerParams(
            collective_id=0, has_side_effects=True, vmem_limit_bytes=63 * 1024 * 1024
        ),
    )(rhs, diagonal, springs, coupling, precond, hub_inverse)


def solution(mesh):
    placed = (
        P("sector", "dof", None),
        P("sector", "dof"),
        P("sector", "dof", None),
        P("sector", "dof"),
        P("dof", None),
        P("dof", None),
    )
    return jax.shard_map(
        body,
        mesh=mesh,
        in_specs=placed,
        out_specs=(P("sector", "dof", None), P("sector", "dof", None)),
        check_vma=False,
    )
```

```python
import jax
import jax.numpy as jnp
from jax import lax
from jax.experimental import pallas as pl
from jax.experimental.pallas import tpu as pltpu
from jax.sharding import PartitionSpec as P

ITERS = 3
NX, NY, NZL, NZH = 4, 8, 2, 4
PARTS = NY * NZL
QUARTER = 64
ROWS = 4 * QUARTER
FACE = 2 * QUARTER
ATT = 3 * QUARTER
HALF = ATT // 2
LOADS = 128
MESH = pl.DeviceIdType.MESH

NEAR = (-1, 1, -2, 2, -3, 3, 4)
COLUMN = len(NEAR)
BLOCKS = 2 * COLUMN + 1


def kernel(
    rhs_hbm, diag_hbm, spring_hbm, couple_hbm, pre_hbm, hub_hbm, sol_ref, res_ref,
    diag_row, spring_row, pre, coup, hubraw, hubblk, rbuf, fbuf, lbuf, qold, qnew, stage,
    v, vec, slopes, image, acc, cacc, hacc, hrecv, load, main, spr, csend, crecv, xsend, xrecv, zsend, zrecv, dsrc, dof_dots, pair_src, pair_dots, all_dots,
    load_sem, r_send, r_sem, f_send, f_sem, n_send, n_sem, c_send, c_sem, x_send, x_sem,
    z_send, z_sem, y_send, y_sem, h_send, h_sem, d_send, d_sem, p_send, p_sem, a_send, a_sem,
):
    s = lax.axis_index("sector")
    d = lax.axis_index("dof")
    zh, x, c = s // (2 * NX), (s // 2) % NX, s % 2
    zl, y = d // NY, d % NY
    plane = zh * NX + x
    nsec = NZH * NX * 2

    def sector_of(zh, x, c):
        return (zh * NX + x) * 2 + c

    def dof_at(column, offset):
        col = zl if column == 0 else 1 - zl
        return col * NY + (y + offset + NY) % NY

    zh_peer = [(sector_of((zh + k) % NZH, x, c), d) for k in range(NZH)]
    x_peer = [(sector_of(zh, (x + j) % NX, c), d) for j in range(NX)]
    dof_peer = [(s, (d + j) % PARTS) for j in range(PARTS)]
    plane_at = [(plane + j) % (NZH * NX) for j in range(NZH * NX)]
    plane_peer = [(m * 2 + c, d) for m in plane_at]
    partner = (s, dof_at(1, 0))
    sibling = (sector_of(zh, x, 1 - c), d)
    next_sec = ((s + 1) % nsec, d)
    prev_sec = ((s + nsec - 1) % nsec, d)

    def send(src, dst, ssem, rsem, dev):
        pltpu.make_async_remote_copy(
            src_ref=src, dst_ref=dst, send_sem=ssem, recv_sem=rsem,
            device_id=dev, device_id_type=MESH,
        ).start()

    def arrived(ref, sem):
        pltpu.make_async_copy(ref, ref, sem).wait()

    loads_in = [
        pltpu.make_async_copy(rhs_hbm, res_ref, load_sem.at[0]),
        pltpu.make_async_copy(pre_hbm, pre, load_sem.at[1]),
        pltpu.make_async_copy(diag_hbm, diag_row, load_sem.at[2]),
        pltpu.make_async_copy(spring_hbm, spring_row, load_sem.at[3]),
        pltpu.make_async_copy(hub_hbm, hubraw, load_sem.at[4]),
        pltpu.make_async_copy(couple_hbm.at[0], coup, load_sem.at[5]),
    ]
    barrier = pltpu.get_barrier_semaphore()
    greet = plane_peer[1:] + dof_peer[1:] + [sibling, next_sec, prev_sec]
    for dev in greet:
        pl.semaphore_signal(barrier, inc=1, device_id=dev, device_id_type=MESH)
    for copy in loads_in:
        copy.start()
    loads_in[0].wait()
    rbuf[d] = res_ref[0].astype(jnp.bfloat16)
    pl.semaphore_wait(barrier, len(greet))

    def begin_gather(buf, ssem, rsem):
        for k, offset in enumerate(NEAR):
            send(buf.at[d], buf.at[d], ssem, rsem.at[k], (s, dof_at(0, -offset)))
        send(buf.at[d], buf.at[d], ssem, rsem.at[COLUMN], partner)

    def take(buf, ssem, rsem, event):
        idx = dof_at(0, NEAR[event])
        arrived(buf.at[idx], rsem.at[event])
        send(buf.at[idx], buf.at[idx], ssem, rsem.at[COLUMN], partner)
        return idx

    across_first = (1 - zl) * NY

    def take_across(buf, rsem):
        arrived(buf.at[pl.ds(across_first, NY)], rsem.at[COLUMN])

    def pre_dot(idx):
        off = pl.multiple_of(idx * ROWS, ROWS)
        return jnp.dot(pre[:, pl.ds(off, ROWS)], rbuf[idx], preferred_element_type=jnp.float32)

    def couple_dot(faces, first, count):
        off = pl.multiple_of(first * FACE, FACE)
        rows = faces[pl.ds(first, count)].reshape(count * FACE, LOADS)
        return jnp.dot(coup[:, pl.ds(off, count * FACE)], rows, preferred_element_type=jnp.float32)

    def ratio(squares, low):
        return jnp.clip(jnp.sqrt(squares / jnp.maximum(low, 1e-30)), 1e-12, 1e12)

    def apply_operator(turn, source, settle, late):
        faces = fbuf.at[turn]
        other = pl.multiple_of((1 - c) * HALF, 8)
        mine = pl.multiple_of(c * HALF, 8)
        csend[...] = spr[pl.ds(other, HALF)] * source[pl.ds(other, HALF)]
        send(csend, crecv, c_send, c_sem, sibling)
        part = spr[pl.ds(mine, HALF)] * source[pl.ds(mine, HALF)]
        arrived(crecv, c_sem)
        part = part + crecv[...]
        xsend[...] = part
        for j in range(1, NX):
            send(xsend, xrecv.at[turn, j], x_send, x_sem.at[turn], x_peer[j])
        arrived(xrecv.at[turn, pl.ds(1, NX - 1)], x_sem.at[turn])
        part = part + xrecv[turn, 1] + xrecv[turn, 2] + xrecv[turn, 3]
        zsend[...] = part
        for k in range(1, NZH):
            send(zsend, zrecv.at[turn, k], z_send, z_sem.at[turn], zh_peer[k])
        alpha = settle()
        stage[...] = vec[:FACE].astype(jnp.bfloat16)
        right, left = pl.ds(QUARTER, QUARTER), pl.ds(0, QUARTER)
        send(stage.at[right], faces.at[d, left], n_send, n_sem.at[turn, 0], next_sec)
        send(stage.at[left], faces.at[d, right], n_send, n_sem.at[turn, 1], prev_sec)
        late(alpha)
        arrived(faces.at[d, left], n_sem.at[turn, 0])
        arrived(faces.at[d, right], n_sem.at[turn, 1])
        begin_gather(faces, f_send, f_sem)
        cacc[...] = couple_dot(faces, d, 1)
        arrived(zrecv.at[turn, pl.ds(1, NZH - 1)], z_sem.at[turn])
        part = part + zrecv[turn, 1] + zrecv[turn, 2] + zrecv[turn, 3]
        part = load[...] + alpha * part
        load[...] = part
        lbuf[d] = part.astype(jnp.bfloat16)
        begin_gather(lbuf, y_send, y_sem)
        for event in range(COLUMN):
            cacc[...] += couple_dot(faces, take(faces, f_send, f_sem, event), 1)
        for event in range(COLUMN):
            take(lbuf, y_send, y_sem, event)
        take_across(faces, f_sem)
        acc[...] = main[...] * vec[...] + cacc[...] + couple_dot(faces, across_first, NY)
        arrived(csend, c_send)
        arrived(stage, n_send)
        arrived(xrecv.at[turn, pl.ds(0, NX - 1)], x_send)
        arrived(faces.at[pl.ds(0, BLOCKS)], f_send)
        arrived(zrecv.at[turn, pl.ds(0, NZH - 1)], z_send)
        take_across(lbuf, y_sem)
        rows = lbuf[...].reshape(PARTS * HALF, LOADS)
        hacc[...] = jnp.dot(hubblk[...], rows, preferred_element_type=jnp.float32)
        send(hacc, hrecv, h_send, h_sem, sibling)
        arrived(hrecv, h_sem)
        acc[:ATT] = acc[:ATT] - spr[...] * (hacc[...] + hrecv[...])
        arrived(hacc, h_send)
        arrived(lbuf.at[pl.ds(0, BLOCKS)], y_send)

    def column_sum(a):
        return jnp.sum(a, axis=0, keepdims=True)

    def dots_begin():
        for j in range(1, PARTS):
            send(dsrc, dof_dots.at[d], d_send, d_sem, dof_peer[j])
        dof_dots[d] = dsrc[...]

    def dots_pair():
        arrived(dof_dots.at[pl.ds(0, PARTS - 1)], d_sem)
        pair_src[...] = jnp.sum(dof_dots[...], axis=0)
        send(pair_src, pair_dots, p_send, p_sem, sibling)

    def dots_plane(turn):
        arrived(pair_dots, p_sem)
        dots = all_dots.at[turn]
        dots[plane] = pair_src[...] + pair_dots[...]
        for j in range(1, NZH * NX):
            send(dots.at[plane], dots.at[plane], a_send, a_sem.at[turn], plane_peer[j])

    def dots_end(turn):
        arrived(all_dots.at[turn, pl.ds(0, NZH * NX - 1)], a_sem.at[turn])
        total = jnp.sum(all_dots[turn], axis=0)
        arrived(dof_dots.at[pl.ds(0, PARTS - 1)], d_send)
        arrived(pair_src, p_send)
        arrived(all_dots.at[turn, pl.ds(0, NZH * NX - 1)], a_send)
        return total[0:1] / (total[1:2] + 1e-06)

    def local_dots():
        im, res = image[...], res_ref[0]
        low, squares = column_sum(im * im), column_sum(res * res)
        dsrc[0:1] = column_sum(im * res)
        dsrc[1:2] = low
        dsrc[2:3] = squares
        return ratio(squares, low)

    def advance(alpha):
        sol_ref[0] = sol_ref[0] + alpha * v[...]
        res_ref[0] = res_ref[0] - alpha * image[...]

    begin_gather(rbuf, r_send, r_sem)
    for copy in loads_in[1:]:
        copy.wait()
    sp = jnp.broadcast_to(spring_row[...], (LOADS, ATT)).T
    spr[...] = sp
    main[...] = jnp.broadcast_to(diag_row[...], (LOADS, ROWS)).T
    main[:ATT] = main[:ATT] + sp
    sol_ref[0] = jnp.zeros((ROWS, LOADS), jnp.float32)
    dsrc[...] = jnp.zeros(dsrc.shape, jnp.float32)

    def first(idx):
        qold[idx] = pre_dot(idx)

    first(d)
    for event in range(COLUMN):
        first(take(rbuf, r_send, r_sem, event))
    for core in range(2):
        @pl.when(c == core)
        def _():
            for k in range(PARTS):
                at, to = k * ATT + core * HALF, k * HALF
                hubblk[:, to:to + HALF] = hubraw[:, at:at + HALF]
    take_across(rbuf, r_sem)
    for k in range(NY):
        first(across_first + k)
    total = qold[0]
    for k in range(1, PARTS):
        total = total + qold[k]
    vec[...] = total
    v[...] = total
    arrived(rbuf.at[pl.ds(0, BLOCKS)], r_send)
    load[...] = jnp.zeros((HALF, LOADS), jnp.float32)
    apply_operator(0, vec, lambda: 1.0, lambda alpha: None)
    image[...] = acc[...]

    def step(it, carry):
        turn = it % 2
        trial = local_dots()
        dots_begin()
        rbuf[d] = (res_ref[0] - trial * image[...]).astype(jnp.bfloat16)
        begin_gather(rbuf, r_send, r_sem)
        qnew[d] = pre_dot(d)
        for event in range(COLUMN):
            idx = take(rbuf, r_send, r_sem, event)
            qnew[idx] = pre_dot(idx)
            if event == 3:
                dots_pair()
            if event == 5:
                dots_plane(turn)

        def slope(idx, product):
            diff = (product - qold[idx]) / ratio(dof_dots[idx, 2:3], dof_dots[idx, 1:2])
            qnew[idx] = diff
            return diff

        total = jnp.zeros((ROWS, LOADS), jnp.float32)
        for k in range(NY):
            total = total + slope(zl * NY + k, qnew[zl * NY + k])
        take_across(rbuf, r_sem)
        for k in range(NY):
            total = total + slope(across_first + k, pre_dot(across_first + k))
        arrived(rbuf.at[pl.ds(0, BLOCKS)], r_send)
        slopes[...] = total

        def settle():
            alpha = dots_end(turn)
            vec[...] = v[...] + alpha * slopes[...]
            return alpha

        def late(alpha):
            advance(alpha)
            v[...] = vec[...]
            for k in range(PARTS):
                qold[k] = qold[k] + alpha * qnew[k]

        apply_operator((it + 1) % 2, slopes, settle, late)
        image[...] = acc[...]
        return carry

    lax.fori_loop(0, ITERS - 1, step, 0)
    last = (ITERS - 1) % 2
    local_dots()
    dots_begin()
    dots_pair()
    dots_plane(last)
    advance(dots_end(last))


def body(rhs, diagonal, coupling, springs, precond, hub_inverse):
    vm = pl.BlockSpec(memory_space=pltpu.VMEM)
    hbm = pl.BlockSpec(memory_space=pltpu.HBM)
    f32, bf16 = jnp.float32, jnp.bfloat16
    dma = pltpu.SemaphoreType.DMA
    mem = pltpu.VMEM
    return pl.pallas_call(
        kernel,
        out_shape=(
            jax.ShapeDtypeStruct((1, ROWS, LOADS), f32),
            jax.ShapeDtypeStruct((1, ROWS, LOADS), f32),
        ),
        in_specs=[hbm] * 6,
        out_specs=(vm, vm),
        scratch_shapes=[
            mem((1, ROWS), f32),
            mem((1, ATT), f32),
            mem((ROWS, PARTS * ROWS), bf16),
            mem((ROWS, PARTS * FACE), bf16),
            mem((ATT, PARTS * ATT), bf16),
            mem((ATT, PARTS * HALF), bf16),
            mem((PARTS, ROWS, LOADS), bf16),
            mem((2, PARTS, FACE, LOADS), bf16),
            mem((PARTS, HALF, LOADS), bf16),
            mem((PARTS, ROWS, LOADS), f32),
            mem((PARTS, ROWS, LOADS), f32),
            mem((FACE, LOADS), bf16),
            mem((ROWS, LOADS), f32),
            mem((ROWS, LOADS), f32),
            mem((ROWS, LOADS), f32),
            mem((ROWS, LOADS), f32),
            mem((ROWS, LOADS), f32),
            mem((ROWS, LOADS), f32),
            mem((ATT, LOADS), f32),
            mem((ATT, LOADS), f32),
            mem((HALF, LOADS), f32),
            mem((ROWS, LOADS), f32),
            mem((ATT, LOADS), f32),
            mem((HALF, LOADS), f32),
            mem((HALF, LOADS), f32),
            mem((HALF, LOADS), f32),
            mem((2, NX, HALF, LOADS), f32),
            mem((HALF, LOADS), f32),
            mem((2, NZH, HALF, LOADS), f32),
            mem((8, LOADS), f32),
            mem((PARTS, 8, LOADS), f32),
            mem((8, LOADS), f32),
            mem((8, LOADS), f32),
            mem((2, NZH * NX, 8, LOADS), f32),
            dma((6,)),
            dma, dma((COLUMN + 1,)),
            dma, dma((COLUMN + 1,)),
            dma, dma((2, 2)),
            dma, dma,
            dma, dma((2,)),
            dma, dma((2,)),
            dma, dma((COLUMN + 1,)),
            dma, dma,
            dma, dma,
            dma, dma,
            dma, dma((2,)),
        ],
        compiler_params=pltpu.CompilerParams(
            collective_id=0, has_side_effects=True, vmem_limit_bytes=61 * 1024 * 1024
        ),
    )(rhs, diagonal, springs, coupling, precond, hub_inverse)


def solution(mesh):
    placed = (
        P("sector", "dof", None),
        P("sector", "dof"),
        P("sector", "dof", None),
        P("sector", "dof"),
        P("dof", None),
        P("dof", None),
    )
    return jax.shard_map(
        body,
        mesh=mesh,
        in_specs=placed,
        out_specs=(P("sector", "dof", None), P("sector", "dof", None)),
        check_vma=False,
    )
```

```python
import jax
import jax.numpy as jnp
from jax import lax
from jax.experimental import pallas as pl
from jax.experimental.pallas import tpu as pltpu
from jax.sharding import PartitionSpec as P

ITERS = 3
NX, NY, NZL, NZH = 4, 8, 2, 4
PARTS = NY * NZL
QUARTER = 64
ROWS = 4 * QUARTER
FACE = 2 * QUARTER
ATT = 3 * QUARTER
HALF = ATT // 2
LOADS = 128
MESH = pl.DeviceIdType.MESH

NEAR = (-1, 1, -2, 2, -3, 3, 4)
COLUMN = len(NEAR)
BLOCKS = 2 * COLUMN + 1


def kernel(
    rhs_hbm, diag_hbm, spring_hbm, couple_hbm, pre_hbm, hub_hbm, sol_ref, res_ref,
    diag_row, spring_row, pre, coup, hubraw, hubblk, rbuf, fbuf, lbuf, qold, qnew, stage,
    v, vec, slopes, inverse, image, acc, cacc, hacc, hrecv, load, main, spr, csend, crecv, xsend, xrecv, zsend, zrecv, dsrc, dof_dots, pair_src, pair_dots, all_dots,
    load_sem, r_send, r_sem, f_send, f_sem, n_send, n_sem, c_send, c_sem, x_send, x_sem,
    z_send, z_sem, y_send, y_sem, h_send, h_sem, d_send, d_sem, p_send, p_sem, a_send, a_sem,
):
    s = lax.axis_index("sector")
    d = lax.axis_index("dof")
    zh, x, c = s // (2 * NX), (s // 2) % NX, s % 2
    zl, y = d // NY, d % NY
    plane = zh * NX + x
    nsec = NZH * NX * 2

    def sector_of(zh, x, c):
        return (zh * NX + x) * 2 + c

    def dof_at(column, offset):
        col = zl if column == 0 else 1 - zl
        return col * NY + (y + offset + NY) % NY

    zh_peer = [(sector_of((zh + k) % NZH, x, c), d) for k in range(NZH)]
    x_peer = [(sector_of(zh, (x + j) % NX, c), d) for j in range(NX)]
    dof_peer = [(s, (d + j) % PARTS) for j in range(PARTS)]
    plane_at = [(plane + j) % (NZH * NX) for j in range(NZH * NX)]
    plane_peer = [(m * 2 + c, d) for m in plane_at]
    partner = (s, dof_at(1, 0))
    sibling = (sector_of(zh, x, 1 - c), d)
    next_sec = ((s + 1) % nsec, d)
    prev_sec = ((s + nsec - 1) % nsec, d)

    def send(src, dst, ssem, rsem, dev):
        pltpu.make_async_remote_copy(
            src_ref=src, dst_ref=dst, send_sem=ssem, recv_sem=rsem,
            device_id=dev, device_id_type=MESH,
        ).start()

    def arrived(ref, sem):
        pltpu.make_async_copy(ref, ref, sem).wait()

    loads_in = [
        pltpu.make_async_copy(rhs_hbm, res_ref, load_sem.at[0]),
        pltpu.make_async_copy(pre_hbm, pre, load_sem.at[1]),
        pltpu.make_async_copy(diag_hbm, diag_row, load_sem.at[2]),
        pltpu.make_async_copy(spring_hbm, spring_row, load_sem.at[3]),
        pltpu.make_async_copy(hub_hbm, hubraw, load_sem.at[4]),
        pltpu.make_async_copy(couple_hbm.at[0], coup, load_sem.at[5]),
    ]
    barrier = pltpu.get_barrier_semaphore()
    greet = plane_peer[1:] + dof_peer[1:] + [sibling, next_sec, prev_sec]
    for dev in greet:
        pl.semaphore_signal(barrier, inc=1, device_id=dev, device_id_type=MESH)
    for copy in loads_in:
        copy.start()
    loads_in[0].wait()
    rbuf[d] = res_ref[0].astype(jnp.bfloat16)
    pl.semaphore_wait(barrier, len(greet))

    def begin_gather(buf, ssem, rsem):
        for k, offset in enumerate(NEAR):
            send(buf.at[d], buf.at[d], ssem, rsem.at[k], (s, dof_at(0, -offset)))
        send(buf.at[d], buf.at[d], ssem, rsem.at[COLUMN], partner)

    def take(buf, ssem, rsem, event, onward=COLUMN):
        idx = dof_at(0, NEAR[event])
        arrived(buf.at[idx], rsem.at[event])
        send(buf.at[idx], buf.at[idx], ssem, rsem.at[onward], partner)
        return idx

    def take_one_across(event):
        idx = dof_at(1, ((0,) + NEAR)[event])
        arrived(rbuf.at[idx], r_sem.at[COLUMN + event])
        return idx

    across_first = (1 - zl) * NY

    def take_across(buf, rsem):
        arrived(buf.at[pl.ds(across_first, NY)], rsem.at[COLUMN])

    def pre_dot(idx):
        off = pl.multiple_of(idx * ROWS, ROWS)
        return jnp.dot(pre[:, pl.ds(off, ROWS)], rbuf[idx], preferred_element_type=jnp.float32)

    def couple_dot(faces, first, count):
        off = pl.multiple_of(first * FACE, FACE)
        rows = faces[pl.ds(first, count)].reshape(count * FACE, LOADS)
        return jnp.dot(coup[:, pl.ds(off, count * FACE)], rows, preferred_element_type=jnp.float32)

    def ratio(squares, low):
        return jnp.clip(jnp.sqrt(squares / jnp.maximum(low, 1e-30)), 1e-12, 1e12)

    def apply_operator(turn, source, settle, late):
        faces = fbuf.at[turn]
        right, left = pl.ds(QUARTER, QUARTER), pl.ds(0, QUARTER)

        def send_faces():
            stage[...] = vec[:FACE].astype(jnp.bfloat16)
            send(stage.at[right], faces.at[d, left], n_send, n_sem.at[turn, 0], next_sec)
            send(stage.at[left], faces.at[d, right], n_send, n_sem.at[turn, 1], prev_sec)

        def gather_faces():
            arrived(faces.at[d, left], n_sem.at[turn, 0])
            arrived(faces.at[d, right], n_sem.at[turn, 1])
            begin_gather(faces, f_send, f_sem)

        def face(event):
            cacc[...] += couple_dot(faces, take(faces, f_send, f_sem, event), 1)

        other = pl.multiple_of((1 - c) * HALF, 8)
        mine = pl.multiple_of(c * HALF, 8)
        csend[...] = spr[pl.ds(other, HALF)] * source[pl.ds(other, HALF)]
        send(csend, crecv, c_send, c_sem, sibling)
        if settle is None:
            send_faces()
        part = spr[pl.ds(mine, HALF)] * source[pl.ds(mine, HALF)]
        arrived(crecv, c_sem)
        part = part + crecv[...]
        xsend[...] = part
        for j in range(1, NX):
            send(xsend, xrecv.at[turn, j], x_send, x_sem.at[turn], x_peer[j])
        if settle is None:
            gather_faces()
        arrived(xrecv.at[turn, pl.ds(1, NX - 1)], x_sem.at[turn])
        part = part + xrecv[turn, 1] + xrecv[turn, 2] + xrecv[turn, 3]
        zsend[...] = part
        for k in range(1, NZH):
            send(zsend, zrecv.at[turn, k], z_send, z_sem.at[turn], zh_peer[k])
        ahead = 0
        if settle is None:
            cacc[...] = couple_dot(faces, d, 1)
            for event in range(COLUMN):
                face(event)
            ahead = COLUMN
        else:
            alpha = settle()
            send_faces()
            late(alpha)
            gather_faces()
            cacc[...] = couple_dot(faces, d, 1)
        arrived(zrecv.at[turn, pl.ds(1, NZH - 1)], z_sem.at[turn])
        part = part + zrecv[turn, 1] + zrecv[turn, 2] + zrecv[turn, 3]
        if settle is not None:
            part = load[...] + alpha * part
        load[...] = part
        lbuf[d] = part.astype(jnp.bfloat16)
        begin_gather(lbuf, y_send, y_sem)
        for event in range(ahead, 4):
            face(event)
        for event in range(COLUMN):
            take(lbuf, y_send, y_sem, event)
            if max(ahead, 4) <= event + 4 < COLUMN:
                face(event + 4)
        take_across(faces, f_sem)
        acc[...] = main[...] * vec[...] + cacc[...] + couple_dot(faces, across_first, NY)
        arrived(csend, c_send)
        arrived(stage, n_send)
        arrived(xrecv.at[turn, pl.ds(0, NX - 1)], x_send)
        arrived(faces.at[pl.ds(0, BLOCKS)], f_send)
        arrived(zrecv.at[turn, pl.ds(0, NZH - 1)], z_send)
        take_across(lbuf, y_sem)
        rows = lbuf[...].reshape(PARTS * HALF, LOADS)
        hacc[...] = jnp.dot(hubblk[...], rows, preferred_element_type=jnp.float32)
        send(hacc, hrecv, h_send, h_sem, sibling)
        arrived(hrecv, h_sem)
        acc[:ATT] = acc[:ATT] - spr[...] * (hacc[...] + hrecv[...])
        arrived(hacc, h_send)
        arrived(lbuf.at[pl.ds(0, BLOCKS)], y_send)

    def column_sum(a):
        return jnp.sum(a, axis=0, keepdims=True)

    def dots_begin():
        for j in range(1, PARTS):
            send(dsrc, dof_dots.at[d], d_send, d_sem, dof_peer[j])
        dof_dots[d] = dsrc[...]

    def dots_pair():
        arrived(dof_dots.at[pl.ds(0, PARTS - 1)], d_sem)
        pair_src[...] = jnp.sum(dof_dots[...], axis=0)
        send(pair_src, pair_dots, p_send, p_sem, sibling)

    def dots_plane(turn):
        arrived(pair_dots, p_sem)
        dots = all_dots.at[turn]
        dots[plane] = pair_src[...] + pair_dots[...]
        for j in range(1, NZH * NX):
            send(dots.at[plane], dots.at[plane], a_send, a_sem.at[turn], plane_peer[j])

    def dots_end(turn):
        arrived(all_dots.at[turn, pl.ds(0, NZH * NX - 1)], a_sem.at[turn])
        total = jnp.sum(all_dots[turn], axis=0)
        arrived(dof_dots.at[pl.ds(0, PARTS - 1)], d_send)
        arrived(pair_src, p_send)
        arrived(all_dots.at[turn, pl.ds(0, NZH * NX - 1)], a_send)
        return total[0:1] / (total[1:2] + 1e-06)

    def local_dots():
        im, res = image[...], res_ref[0]
        low, squares = column_sum(im * im), column_sum(res * res)
        dsrc[0:1] = column_sum(im * res)
        dsrc[1:2] = low
        dsrc[2:3] = squares
        return ratio(squares, low)

    def advance(alpha):
        sol_ref[0] = sol_ref[0] + alpha * v[...]
        res_ref[0] = res_ref[0] - alpha * image[...]

    begin_gather(rbuf, r_send, r_sem)
    for copy in loads_in[1:]:
        copy.wait()
    sp = jnp.broadcast_to(spring_row[...], (LOADS, ATT)).T
    spr[...] = sp
    main[...] = jnp.broadcast_to(diag_row[...], (LOADS, ROWS)).T
    main[:ATT] = main[:ATT] + sp
    sol_ref[0] = jnp.zeros((ROWS, LOADS), jnp.float32)
    dsrc[...] = jnp.zeros(dsrc.shape, jnp.float32)

    def first(idx):
        qold[idx] = pre_dot(idx)

    first(d)
    for event in range(COLUMN):
        first(take(rbuf, r_send, r_sem, event, COLUMN + 1 + event))
    for core in range(2):
        @pl.when(c == core)
        def _():
            for k in range(PARTS):
                at, to = k * ATT + core * HALF, k * HALF
                hubblk[:, to:to + HALF] = hubraw[:, at:at + HALF]
    total = qold[zl * NY]
    for k in range(1, NY):
        total = total + qold[zl * NY + k]
    vec[...] = total
    for event in range(NY):
        idx = take_one_across(event)
        product = pre_dot(idx)
        qold[idx] = product
        vec[...] += product
    v[...] = vec[...]
    arrived(rbuf.at[pl.ds(0, BLOCKS)], r_send)
    apply_operator(0, vec, None, None)
    image[...] = acc[...]

    def step(it, carry):
        turn = it % 2
        trial = local_dots()
        rbuf[d] = (res_ref[0] - trial * image[...]).astype(jnp.bfloat16)
        begin_gather(rbuf, r_send, r_sem)
        dots_begin()
        qnew[d] = pre_dot(d)
        for event in range(COLUMN):
            idx = take(rbuf, r_send, r_sem, event, COLUMN + 1 + event)
            qnew[idx] = pre_dot(idx)
            if event == 4:
                dots_pair()
        dots_plane(turn)
        inverse[...] = 1.0 / ratio(dof_dots[:, 2, :], dof_dots[:, 1, :])

        def slope(idx, product):
            diff = (product - qold[idx]) * inverse[pl.ds(idx, 1)]
            qnew[idx] = diff
            return diff

        total = jnp.zeros((ROWS, LOADS), jnp.float32)
        for k in range(NY):
            total = total + slope(zl * NY + k, qnew[zl * NY + k])
        slopes[...] = total
        for event in range(NY):
            idx = take_one_across(event)
            slopes[...] += slope(idx, pre_dot(idx))
        arrived(rbuf.at[pl.ds(0, BLOCKS)], r_send)

        def settle():
            alpha = dots_end(turn)
            vec[...] = v[...] + alpha * slopes[...]
            return alpha

        def late(alpha):
            advance(alpha)
            v[...] = vec[...]
            for k in range(PARTS):
                qold[k] = qold[k] + alpha * qnew[k]

        apply_operator((it + 1) % 2, slopes, settle, late)
        image[...] = acc[...]
        return carry

    lax.fori_loop(0, ITERS - 1, step, 0)
    last = (ITERS - 1) % 2
    local_dots()
    dots_begin()
    dots_pair()
    dots_plane(last)
    advance(dots_end(last))


def body(rhs, diagonal, coupling, springs, precond, hub_inverse):
    vm = pl.BlockSpec(memory_space=pltpu.VMEM)
    hbm = pl.BlockSpec(memory_space=pltpu.HBM)
    f32, bf16 = jnp.float32, jnp.bfloat16
    dma = pltpu.SemaphoreType.DMA
    mem = pltpu.VMEM
    return pl.pallas_call(
        kernel,
        out_shape=(
            jax.ShapeDtypeStruct((1, ROWS, LOADS), f32),
            jax.ShapeDtypeStruct((1, ROWS, LOADS), f32),
        ),
        in_specs=[hbm] * 6,
        out_specs=(vm, vm),
        scratch_shapes=[
            mem((1, ROWS), f32),
            mem((1, ATT), f32),
            mem((ROWS, PARTS * ROWS), bf16),
            mem((ROWS, PARTS * FACE), bf16),
            mem((ATT, PARTS * ATT), bf16),
            mem((ATT, PARTS * HALF), bf16),
            mem((PARTS, ROWS, LOADS), bf16),
            mem((2, PARTS, FACE, LOADS), bf16),
            mem((PARTS, HALF, LOADS), bf16),
            mem((PARTS, ROWS, LOADS), f32),
            mem((PARTS, ROWS, LOADS), f32),
            mem((FACE, LOADS), bf16),
            mem((ROWS, LOADS), f32),
            mem((ROWS, LOADS), f32),
            mem((ROWS, LOADS), f32),
            mem((PARTS, LOADS), f32),
            mem((ROWS, LOADS), f32),
            mem((ROWS, LOADS), f32),
            mem((ROWS, LOADS), f32),
            mem((ATT, LOADS), f32),
            mem((ATT, LOADS), f32),
            mem((HALF, LOADS), f32),
            mem((ROWS, LOADS), f32),
            mem((ATT, LOADS), f32),
            mem((HALF, LOADS), f32),
            mem((HALF, LOADS), f32),
            mem((HALF, LOADS), f32),
            mem((2, NX, HALF, LOADS), f32),
            mem((HALF, LOADS), f32),
            mem((2, NZH, HALF, LOADS), f32),
            mem((8, LOADS), f32),
            mem((PARTS, 8, LOADS), f32),
            mem((8, LOADS), f32),
            mem((8, LOADS), f32),
            mem((2, NZH * NX, 8, LOADS), f32),
            dma((6,)),
            dma, dma((BLOCKS,)),
            dma, dma((COLUMN + 1,)),
            dma, dma((2, 2)),
            dma, dma,
            dma, dma((2,)),
            dma, dma((2,)),
            dma, dma((COLUMN + 1,)),
            dma, dma,
            dma, dma,
            dma, dma,
            dma, dma((2,)),
        ],
        compiler_params=pltpu.CompilerParams(
            collective_id=0, has_side_effects=True, vmem_limit_bytes=61 * 1024 * 1024
        ),
    )(rhs, diagonal, springs, coupling, precond, hub_inverse)


def solution(mesh):
    placed = (
        P("sector", "dof", None),
        P("sector", "dof"),
        P("sector", "dof", None),
        P("sector", "dof"),
        P("dof", None),
        P("dof", None),
    )
    return jax.shard_map(
        body,
        mesh=mesh,
        in_specs=placed,
        out_specs=(P("sector", "dof", None), P("sector", "dof", None)),
        check_vma=False,
    )
```

```python
import jax
import jax.numpy as jnp
from jax import lax
from jax.experimental import pallas as pl
from jax.experimental.pallas import tpu as pltpu
from jax.sharding import PartitionSpec as P

ITERS = 3
NX, NY, NZL, NZH = 4, 8, 2, 4
PARTS = NY * NZL
QUARTER = 64
ROWS = 4 * QUARTER
FACE = 2 * QUARTER
ATT = 3 * QUARTER
HALF = ATT // 2
LOADS = 128
MESH = pl.DeviceIdType.MESH

NEAR = (-2, 2, -1, 1, -3, 3, -4)
COLUMN = len(NEAR)
BLOCKS = 2 * COLUMN + 1


def kernel(
    rhs_hbm, diag_hbm, spring_hbm, couple_hbm, pre_hbm, hub_hbm, sol_ref, res_ref,
    diag_row, spring_row, pre, coup, hubraw, hubblk, rbuf, fbuf, lbuf, qold, qnew, stage,
    v, vec, slopes, inverse, image, acc, cacc, hacc, hrecv, load, main, spr, csend, crecv, xsend, xrecv, zsend, zrecv, dsrc, dof_dots, pair_src, pair_dots, all_dots,
    load_sem, r_send, r_sem, f_send, f_sem, n_send, n_sem, c_send, c_sem, x_send, x_sem,
    z_send, z_sem, y_send, y_sem, h_send, h_sem, d_send, d_sem, p_send, p_sem, a_send, a_sem,
):
    s = lax.axis_index("sector")
    d = lax.axis_index("dof")
    zh, x, c = s // (2 * NX), (s // 2) % NX, s % 2
    zl, y = d // NY, d % NY
    plane = zh * NX + x
    nsec = NZH * NX * 2

    def sector_of(zh, x, c):
        return (zh * NX + x) * 2 + c

    def dof_at(column, offset):
        col = zl if column == 0 else 1 - zl
        return col * NY + (y + offset + NY) % NY

    zh_peer = [(sector_of((zh + k) % NZH, x, c), d) for k in range(NZH)]
    x_peer = [(sector_of(zh, (x + j) % NX, c), d) for j in range(NX)]
    dof_peer = [(s, (d + j) % PARTS) for j in range(PARTS)]
    plane_at = [(plane + j) % (NZH * NX) for j in range(NZH * NX)]
    plane_peer = [(m * 2 + c, d) for m in plane_at]
    partner = (s, dof_at(1, 0))
    sibling = (sector_of(zh, x, 1 - c), d)
    next_sec = ((s + 1) % nsec, d)
    prev_sec = ((s + nsec - 1) % nsec, d)

    def send(src, dst, ssem, rsem, dev):
        pltpu.make_async_remote_copy(
            src_ref=src, dst_ref=dst, send_sem=ssem, recv_sem=rsem,
            device_id=dev, device_id_type=MESH,
        ).start()

    def arrived(ref, sem):
        pltpu.make_async_copy(ref, ref, sem).wait()

    loads_in = [
        pltpu.make_async_copy(rhs_hbm, res_ref, load_sem.at[0]),
        pltpu.make_async_copy(pre_hbm, pre, load_sem.at[1]),
        pltpu.make_async_copy(diag_hbm, diag_row, load_sem.at[2]),
        pltpu.make_async_copy(spring_hbm, spring_row, load_sem.at[3]),
        pltpu.make_async_copy(hub_hbm, hubraw, load_sem.at[4]),
        pltpu.make_async_copy(couple_hbm.at[0], coup, load_sem.at[5]),
    ]
    barrier = pltpu.get_barrier_semaphore()
    greet = plane_peer[1:] + dof_peer[1:] + [sibling, next_sec, prev_sec]
    for dev in greet:
        pl.semaphore_signal(barrier, inc=1, device_id=dev, device_id_type=MESH)
    for copy in loads_in:
        copy.start()
    loads_in[0].wait()
    rbuf[d] = res_ref[0].astype(jnp.bfloat16)
    pl.semaphore_wait(barrier, len(greet))

    def begin_gather(buf, ssem, rsem):
        for k, offset in enumerate(NEAR[:-1]):
            send(buf.at[d], buf.at[d], ssem, rsem.at[k], (s, dof_at(0, -offset)))
        send(buf.at[d], buf.at[d], ssem, rsem.at[COLUMN], partner)

    def take(buf, ssem, rsem, event, onward=COLUMN):
        idx = dof_at(0, NEAR[event])
        arrived(buf.at[idx], rsem.at[event])
        if event == 0:
            send(buf.at[idx], buf.at[idx], ssem, rsem.at[COLUMN - 1], (s, dof_at(0, 2)))
        send(buf.at[idx], buf.at[idx], ssem, rsem.at[onward], partner)
        return idx

    def take_one_across(event):
        idx = dof_at(1, ((0,) + NEAR)[event])
        arrived(rbuf.at[idx], r_sem.at[COLUMN + event])
        return idx

    across_first = (1 - zl) * NY

    def take_across(buf, rsem):
        arrived(buf.at[pl.ds(across_first, NY)], rsem.at[COLUMN])

    def pre_dot(idx):
        off = pl.multiple_of(idx * ROWS, ROWS)
        return jnp.dot(pre[:, pl.ds(off, ROWS)], rbuf[idx], preferred_element_type=jnp.float32)

    def couple_dot(faces, first, count):
        off = pl.multiple_of(first * FACE, FACE)
        rows = faces[pl.ds(first, count)].reshape(count * FACE, LOADS)
        return jnp.dot(coup[:, pl.ds(off, count * FACE)], rows, preferred_element_type=jnp.float32)

    def ratio(squares, low):
        return jnp.clip(jnp.sqrt(squares / jnp.maximum(low, 1e-30)), 1e-12, 1e12)

    def apply_operator(turn, source, settle, late):
        faces = fbuf.at[turn]
        right, left = pl.ds(QUARTER, QUARTER), pl.ds(0, QUARTER)

        def send_faces():
            stage[...] = vec[:FACE].astype(jnp.bfloat16)
            send(stage.at[right], faces.at[d, left], n_send, n_sem.at[turn, 0], next_sec)
            send(stage.at[left], faces.at[d, right], n_send, n_sem.at[turn, 1], prev_sec)

        def gather_faces():
            arrived(faces.at[d, left], n_sem.at[turn, 0])
            arrived(faces.at[d, right], n_sem.at[turn, 1])
            begin_gather(faces, f_send, f_sem)

        def face(event):
            cacc[...] += couple_dot(faces, take(faces, f_send, f_sem, event), 1)

        other = pl.multiple_of((1 - c) * HALF, 8)
        mine = pl.multiple_of(c * HALF, 8)
        csend[...] = spr[pl.ds(other, HALF)] * source[pl.ds(other, HALF)]
        send(csend, crecv, c_send, c_sem, sibling)
        if settle is None:
            send_faces()
        part = spr[pl.ds(mine, HALF)] * source[pl.ds(mine, HALF)]
        arrived(crecv, c_sem)
        part = part + crecv[...]
        xsend[...] = part
        for j in range(1, NX):
            send(xsend, xrecv.at[turn, j], x_send, x_sem.at[turn], x_peer[j])
        if settle is None:
            gather_faces()
        arrived(xrecv.at[turn, pl.ds(1, NX - 1)], x_sem.at[turn])
        part = part + xrecv[turn, 1] + xrecv[turn, 2] + xrecv[turn, 3]
        zsend[...] = part
        for k in range(1, NZH):
            send(zsend, zrecv.at[turn, k], z_send, z_sem.at[turn], zh_peer[k])
        ahead = 0
        if settle is None:
            cacc[...] = couple_dot(faces, d, 1)
            for event in range(COLUMN):
                face(event)
            ahead = COLUMN
        else:
            alpha = settle()
            send_faces()
            late(alpha)
            gather_faces()
            cacc[...] = couple_dot(faces, d, 1)
        arrived(zrecv.at[turn, pl.ds(1, NZH - 1)], z_sem.at[turn])
        part = part + zrecv[turn, 1] + zrecv[turn, 2] + zrecv[turn, 3]
        if settle is not None:
            part = load[...] + alpha * part
        load[...] = part
        lbuf[d] = part.astype(jnp.bfloat16)
        begin_gather(lbuf, y_send, y_sem)
        for event in range(ahead, 4):
            face(event)
        for event in range(COLUMN):
            take(lbuf, y_send, y_sem, event)
            if max(ahead, 4) <= event + 4 < COLUMN:
                face(event + 4)
        take_across(faces, f_sem)
        acc[...] = main[...] * vec[...] + cacc[...] + couple_dot(faces, across_first, NY)
        arrived(csend, c_send)
        arrived(stage, n_send)
        arrived(xrecv.at[turn, pl.ds(0, NX - 1)], x_send)
        arrived(faces.at[pl.ds(0, BLOCKS)], f_send)
        arrived(zrecv.at[turn, pl.ds(0, NZH - 1)], z_send)
        take_across(lbuf, y_sem)
        rows = lbuf[...].reshape(PARTS * HALF, LOADS)
        hacc[...] = jnp.dot(hubblk[...], rows, preferred_element_type=jnp.float32)
        send(hacc, hrecv, h_send, h_sem, sibling)
        arrived(hrecv, h_sem)
        acc[:ATT] = acc[:ATT] - spr[...] * (hacc[...] + hrecv[...])
        arrived(hacc, h_send)
        arrived(lbuf.at[pl.ds(0, BLOCKS)], y_send)

    def column_sum(a):
        return jnp.sum(a, axis=0, keepdims=True)

    def dots_begin():
        for j in range(1, PARTS):
            send(dsrc, dof_dots.at[d], d_send, d_sem, dof_peer[j])
        dof_dots[d] = dsrc[...]

    def dots_pair():
        arrived(dof_dots.at[pl.ds(0, PARTS - 1)], d_sem)
        pair_src[...] = jnp.sum(dof_dots[...], axis=0)
        send(pair_src, pair_dots, p_send, p_sem, sibling)

    def dots_plane(turn):
        arrived(pair_dots, p_sem)
        dots = all_dots.at[turn]
        dots[plane] = pair_src[...] + pair_dots[...]
        for j in range(1, NZH * NX):
            send(dots.at[plane], dots.at[plane], a_send, a_sem.at[turn], plane_peer[j])

    def dots_end(turn):
        arrived(all_dots.at[turn, pl.ds(0, NZH * NX - 1)], a_sem.at[turn])
        total = jnp.sum(all_dots[turn], axis=0)
        arrived(dof_dots.at[pl.ds(0, PARTS - 1)], d_send)
        arrived(pair_src, p_send)
        arrived(all_dots.at[turn, pl.ds(0, NZH * NX - 1)], a_send)
        return total[0:1] / (total[1:2] + 1e-06)

    def local_dots():
        im, res = image[...], res_ref[0]
        low, squares = column_sum(im * im), column_sum(res * res)
        dsrc[0:1] = column_sum(im * res)
        dsrc[1:2] = low
        dsrc[2:3] = squares
        return ratio(squares, low)

    def advance(alpha):
        sol_ref[0] = sol_ref[0] + alpha * v[...]
        res_ref[0] = res_ref[0] - alpha * image[...]

    begin_gather(rbuf, r_send, r_sem)
    for copy in loads_in[1:]:
        copy.wait()
    sp = jnp.broadcast_to(spring_row[...], (LOADS, ATT)).T
    spr[...] = sp
    main[...] = jnp.broadcast_to(diag_row[...], (LOADS, ROWS)).T
    main[:ATT] = main[:ATT] + sp
    sol_ref[0] = jnp.zeros((ROWS, LOADS), jnp.float32)
    dsrc[...] = jnp.zeros(dsrc.shape, jnp.float32)

    def first(idx):
        qold[idx] = pre_dot(idx)

    first(d)
    for event in range(COLUMN):
        first(take(rbuf, r_send, r_sem, event, COLUMN + 1 + event))
    for core in range(2):
        @pl.when(c == core)
        def _():
            for k in range(PARTS):
                at, to = k * ATT + core * HALF, k * HALF
                hubblk[:, to:to + HALF] = hubraw[:, at:at + HALF]
    total = qold[zl * NY]
    for k in range(1, NY):
        total = total + qold[zl * NY + k]
    vec[...] = total
    for event in range(NY):
        idx = take_one_across(event)
        product = pre_dot(idx)
        qold[idx] = product
        vec[...] += product
    v[...] = vec[...]
    arrived(rbuf.at[pl.ds(0, BLOCKS)], r_send)
    apply_operator(0, vec, None, None)
    image[...] = acc[...]

    def step(it, carry):
        turn = it % 2
        trial = local_dots()
        rbuf[d] = (res_ref[0] - trial * image[...]).astype(jnp.bfloat16)
        begin_gather(rbuf, r_send, r_sem)
        dots_begin()
        qnew[d] = pre_dot(d)
        for event in range(COLUMN):
            idx = take(rbuf, r_send, r_sem, event, COLUMN + 1 + event)
            qnew[idx] = pre_dot(idx)
            if event == 4:
                dots_pair()
        dots_plane(turn)
        inverse[...] = 1.0 / ratio(dof_dots[:, 2, :], dof_dots[:, 1, :])

        def slope(idx, product):
            diff = (product - qold[idx]) * inverse[pl.ds(idx, 1)]
            qnew[idx] = diff
            return diff

        total = jnp.zeros((ROWS, LOADS), jnp.float32)
        for k in range(NY):
            total = total + slope(zl * NY + k, qnew[zl * NY + k])
        slopes[...] = total
        for event in range(NY):
            idx = take_one_across(event)
            slopes[...] += slope(idx, pre_dot(idx))
        arrived(rbuf.at[pl.ds(0, BLOCKS)], r_send)

        def settle():
            alpha = dots_end(turn)
            vec[...] = v[...] + alpha * slopes[...]
            return alpha

        def late(alpha):
            advance(alpha)
            v[...] = vec[...]
            for k in range(PARTS):
                qold[k] = qold[k] + alpha * qnew[k]

        apply_operator((it + 1) % 2, slopes, settle, late)
        image[...] = acc[...]
        return carry

    lax.fori_loop(0, ITERS - 1, step, 0)
    last = (ITERS - 1) % 2
    local_dots()
    dots_begin()
    dots_pair()
    dots_plane(last)
    advance(dots_end(last))


def body(rhs, diagonal, coupling, springs, precond, hub_inverse):
    vm = pl.BlockSpec(memory_space=pltpu.VMEM)
    hbm = pl.BlockSpec(memory_space=pltpu.HBM)
    f32, bf16 = jnp.float32, jnp.bfloat16
    dma = pltpu.SemaphoreType.DMA
    mem = pltpu.VMEM
    return pl.pallas_call(
        kernel,
        out_shape=(
            jax.ShapeDtypeStruct((1, ROWS, LOADS), f32),
            jax.ShapeDtypeStruct((1, ROWS, LOADS), f32),
        ),
        in_specs=[hbm] * 6,
        out_specs=(vm, vm),
        scratch_shapes=[
            mem((1, ROWS), f32),
            mem((1, ATT), f32),
            mem((ROWS, PARTS * ROWS), bf16),
            mem((ROWS, PARTS * FACE), bf16),
            mem((ATT, PARTS * ATT), bf16),
            mem((ATT, PARTS * HALF), bf16),
            mem((PARTS, ROWS, LOADS), bf16),
            mem((2, PARTS, FACE, LOADS), bf16),
            mem((PARTS, HALF, LOADS), bf16),
            mem((PARTS, ROWS, LOADS), f32),
            mem((PARTS, ROWS, LOADS), f32),
            mem((FACE, LOADS), bf16),
            mem((ROWS, LOADS), f32),
            mem((ROWS, LOADS), f32),
            mem((ROWS, LOADS), f32),
            mem((PARTS, LOADS), f32),
            mem((ROWS, LOADS), f32),
            mem((ROWS, LOADS), f32),
            mem((ROWS, LOADS), f32),
            mem((ATT, LOADS), f32),
            mem((ATT, LOADS), f32),
            mem((HALF, LOADS), f32),
            mem((ROWS, LOADS), f32),
            mem((ATT, LOADS), f32),
            mem((HALF, LOADS), f32),
            mem((HALF, LOADS), f32),
            mem((HALF, LOADS), f32),
            mem((2, NX, HALF, LOADS), f32),
            mem((HALF, LOADS), f32),
            mem((2, NZH, HALF, LOADS), f32),
            mem((8, LOADS), f32),
            mem((PARTS, 8, LOADS), f32),
            mem((8, LOADS), f32),
            mem((8, LOADS), f32),
            mem((2, NZH * NX, 8, LOADS), f32),
            dma((6,)),
            dma, dma((BLOCKS,)),
            dma, dma((COLUMN + 1,)),
            dma, dma((2, 2)),
            dma, dma,
            dma, dma((2,)),
            dma, dma((2,)),
            dma, dma((COLUMN + 1,)),
            dma, dma,
            dma, dma,
            dma, dma,
            dma, dma((2,)),
        ],
        compiler_params=pltpu.CompilerParams(
            collective_id=0, has_side_effects=True, vmem_limit_bytes=61 * 1024 * 1024
        ),
    )(rhs, diagonal, springs, coupling, precond, hub_inverse)


def solution(mesh):
    placed = (
        P("sector", "dof", None),
        P("sector", "dof"),
        P("sector", "dof", None),
        P("sector", "dof"),
        P("dof", None),
        P("dof", None),
    )
    return jax.shard_map(
        body,
        mesh=mesh,
        in_specs=placed,
        out_specs=(P("sector", "dof", None), P("sector", "dof", None)),
        check_vma=False,
    )
```

```python
import jax
import jax.numpy as jnp
from jax import lax
from jax.experimental import pallas as pl
from jax.experimental.pallas import tpu as pltpu
from jax.sharding import PartitionSpec as P

ITERS = 3
NX, NY, NZL, NZH = 4, 8, 2, 4
PARTS = NY * NZL
QUARTER = 64
ROWS = 4 * QUARTER
FACE = 2 * QUARTER
ATT = 3 * QUARTER
HALF = ATT // 2
LOADS = 128
MESH = pl.DeviceIdType.MESH

NEAR = (-2, 2, -1, 1, -3, 3, -4)
COLUMN = len(NEAR)
BLOCKS = 2 * COLUMN + 1


def kernel(
    rhs_hbm, diag_hbm, spring_hbm, couple_hbm, pre_hbm, hub_hbm, sol_ref, res_ref, v, image,
    diag_row, spring_row, pre, coup, hubraw, hubblk, rbuf, fbuf, lbuf, qold, qnew, stage,
    vec, slopes, inverse, acc, cacc, hacc, hrecv, load, main, spr, csend, crecv, xsend, xrecv, zsend, zrecv, dsrc, dof_dots, pair_src, pair_dots, all_dots,
    load_sem, r_send, r_sem, f_send, f_sem, n_send, n_sem, c_send, c_sem, x_send, x_sem,
    z_send, z_sem, y_send, y_sem, h_send, h_sem, d_send, d_sem, p_send, p_sem, a_send, a_sem,
):
    s = lax.axis_index("sector")
    d = lax.axis_index("dof")
    zh, x, c = s // (2 * NX), (s // 2) % NX, s % 2
    zl, y = d // NY, d % NY
    plane = zh * NX + x
    nsec = NZH * NX * 2

    def sector_of(zh, x, c):
        return (zh * NX + x) * 2 + c

    def dof_at(column, offset):
        col = zl if column == 0 else 1 - zl
        return col * NY + (y + offset + NY) % NY

    zh_peer = [(sector_of((zh + k) % NZH, x, c), d) for k in range(NZH)]
    x_peer = [(sector_of(zh, (x + j) % NX, c), d) for j in range(NX)]
    dof_peer = [(s, (d + j) % PARTS) for j in range(PARTS)]
    plane_at = [(plane + j) % (NZH * NX) for j in range(NZH * NX)]
    plane_peer = [(m * 2 + c, d) for m in plane_at]
    partner = (s, dof_at(1, 0))
    sibling = (sector_of(zh, x, 1 - c), d)
    next_sec = ((s + 1) % nsec, d)
    prev_sec = ((s + nsec - 1) % nsec, d)

    def send(src, dst, ssem, rsem, dev):
        pltpu.make_async_remote_copy(
            src_ref=src, dst_ref=dst, send_sem=ssem, recv_sem=rsem,
            device_id=dev, device_id_type=MESH,
        ).start()

    def arrived(ref, sem):
        pltpu.make_async_copy(ref, ref, sem).wait()

    loads_in = [
        pltpu.make_async_copy(rhs_hbm, res_ref, load_sem.at[0]),
        pltpu.make_async_copy(pre_hbm, pre, load_sem.at[1]),
        pltpu.make_async_copy(diag_hbm, diag_row, load_sem.at[2]),
        pltpu.make_async_copy(spring_hbm, spring_row, load_sem.at[3]),
        pltpu.make_async_copy(hub_hbm, hubraw, load_sem.at[4]),
        pltpu.make_async_copy(couple_hbm.at[0], coup, load_sem.at[5]),
    ]
    barrier = pltpu.get_barrier_semaphore()
    greet = plane_peer[1:] + dof_peer[1:] + [sibling, next_sec, prev_sec]
    for dev in greet:
        pl.semaphore_signal(barrier, inc=1, device_id=dev, device_id_type=MESH)
    for copy in loads_in:
        copy.start()
    loads_in[0].wait()
    rbuf[d] = res_ref[0].astype(jnp.bfloat16)
    pl.semaphore_wait(barrier, len(greet))

    def begin_gather(buf, ssem, rsem):
        for k, offset in enumerate(NEAR[:-1]):
            send(buf.at[d], buf.at[d], ssem, rsem.at[k], (s, dof_at(0, -offset)))
        send(buf.at[d], buf.at[d], ssem, rsem.at[COLUMN], partner)

    def take(buf, ssem, rsem, event, onward=COLUMN):
        idx = dof_at(0, NEAR[event])
        arrived(buf.at[idx], rsem.at[event])
        if event == 0:
            send(buf.at[idx], buf.at[idx], ssem, rsem.at[COLUMN - 1], (s, dof_at(0, 2)))
        send(buf.at[idx], buf.at[idx], ssem, rsem.at[onward], partner)
        return idx

    def take_one_across(event):
        idx = dof_at(1, ((0,) + NEAR)[event])
        arrived(rbuf.at[idx], r_sem.at[COLUMN + event])
        return idx

    across_first = (1 - zl) * NY

    def take_across(buf, rsem):
        arrived(buf.at[pl.ds(across_first, NY)], rsem.at[COLUMN])

    def pre_dot(idx):
        off = pl.multiple_of(idx * ROWS, ROWS)
        return jnp.dot(pre[:, pl.ds(off, ROWS)], rbuf[idx], preferred_element_type=jnp.float32)

    def couple_dot(faces, first, count):
        off = pl.multiple_of(first * FACE, FACE)
        rows = faces[pl.ds(first, count)].reshape(count * FACE, LOADS)
        return jnp.dot(coup[:, pl.ds(off, count * FACE)], rows, preferred_element_type=jnp.float32)

    def ratio(squares, low):
        return jnp.clip(jnp.sqrt(squares / jnp.maximum(low, 1e-30)), 1e-12, 1e12)

    def apply_operator(turn, source, settle, late):
        faces = fbuf.at[turn]
        right, left = pl.ds(QUARTER, QUARTER), pl.ds(0, QUARTER)

        def send_faces():
            stage[...] = vec[:FACE].astype(jnp.bfloat16)
            send(stage.at[right], faces.at[d, left], n_send, n_sem.at[turn, 0], next_sec)
            send(stage.at[left], faces.at[d, right], n_send, n_sem.at[turn, 1], prev_sec)

        def gather_faces():
            arrived(faces.at[d, left], n_sem.at[turn, 0])
            arrived(faces.at[d, right], n_sem.at[turn, 1])
            begin_gather(faces, f_send, f_sem)

        def face(event):
            cacc[...] += couple_dot(faces, take(faces, f_send, f_sem, event), 1)

        other = pl.multiple_of((1 - c) * HALF, 8)
        mine = pl.multiple_of(c * HALF, 8)
        csend[...] = spr[pl.ds(other, HALF)] * source[pl.ds(other, HALF)]
        send(csend, crecv, c_send, c_sem, sibling)
        if settle is None:
            send_faces()
        part = spr[pl.ds(mine, HALF)] * source[pl.ds(mine, HALF)]
        arrived(crecv, c_sem)
        part = part + crecv[...]
        xsend[...] = part
        for j in range(1, NX):
            send(xsend, xrecv.at[turn, j], x_send, x_sem.at[turn], x_peer[j])
        if settle is None:
            gather_faces()
        else:
            alpha = settle()
            send_faces()
            late(alpha)
        arrived(xrecv.at[turn, pl.ds(1, NX - 1)], x_sem.at[turn])
        part = part + xrecv[turn, 1] + xrecv[turn, 2] + xrecv[turn, 3]
        zsend[...] = part
        for k in range(1, NZH):
            send(zsend, zrecv.at[turn, k], z_send, z_sem.at[turn], zh_peer[k])
        ahead = 0
        if settle is None:
            cacc[...] = couple_dot(faces, d, 1)
            for event in range(COLUMN):
                face(event)
            ahead = COLUMN
        else:
            gather_faces()
            cacc[...] = couple_dot(faces, d, 1)
        arrived(zrecv.at[turn, pl.ds(1, NZH - 1)], z_sem.at[turn])
        part = part + zrecv[turn, 1] + zrecv[turn, 2] + zrecv[turn, 3]
        if settle is not None:
            part = load[...] + alpha * part
        load[...] = part
        lbuf[d] = part.astype(jnp.bfloat16)
        begin_gather(lbuf, y_send, y_sem)
        for event in range(ahead, 4):
            face(event)
        for event in range(COLUMN):
            take(lbuf, y_send, y_sem, event)
            if max(ahead, 4) <= event + 4 < COLUMN:
                face(event + 4)
        take_across(faces, f_sem)
        acc[...] = main[...] * vec[...] + cacc[...] + couple_dot(faces, across_first, NY)
        arrived(csend, c_send)
        arrived(stage, n_send)
        arrived(xrecv.at[turn, pl.ds(0, NX - 1)], x_send)
        arrived(faces.at[pl.ds(0, BLOCKS)], f_send)
        arrived(zrecv.at[turn, pl.ds(0, NZH - 1)], z_send)
        take_across(lbuf, y_sem)
        rows = lbuf[...].reshape(PARTS * HALF, LOADS)
        hacc[...] = jnp.dot(hubblk[...], rows, preferred_element_type=jnp.float32)
        send(hacc, hrecv, h_send, h_sem, sibling)
        arrived(hrecv, h_sem)
        acc[:ATT] = acc[:ATT] - spr[...] * (hacc[...] + hrecv[...])
        arrived(hacc, h_send)
        arrived(lbuf.at[pl.ds(0, BLOCKS)], y_send)

    def column_sum(a):
        return jnp.sum(a, axis=0, keepdims=True)

    def dots_begin():
        dsrc[0:1] = column_sum(image[...] * res_ref[0])
        for j in range(1, PARTS):
            send(dsrc, dof_dots.at[d], d_send, d_sem, dof_peer[j])
        dof_dots[d] = dsrc[...]

    def dots_pair():
        arrived(dof_dots.at[pl.ds(0, PARTS - 1)], d_sem)
        pair_src[...] = jnp.sum(dof_dots[...], axis=0)
        send(pair_src, pair_dots, p_send, p_sem, sibling)

    def dots_plane(turn):
        arrived(pair_dots, p_sem)
        dots = all_dots.at[turn]
        dots[plane] = pair_src[...] + pair_dots[...]
        for j in range(1, NZH * NX):
            send(dots.at[plane], dots.at[plane], a_send, a_sem.at[turn], plane_peer[j])

    def dots_end(turn):
        arrived(all_dots.at[turn, pl.ds(0, NZH * NX - 1)], a_sem.at[turn])
        total = jnp.sum(all_dots[turn], axis=0)
        arrived(dof_dots.at[pl.ds(0, PARTS - 1)], d_send)
        arrived(pair_src, p_send)
        arrived(all_dots.at[turn, pl.ds(0, NZH * NX - 1)], a_send)
        return total[0:1] / (total[1:2] + 1e-06)

    def local_dots():
        im, res = image[...], res_ref[0]
        low, squares = column_sum(im * im), column_sum(res * res)
        dsrc[1:2] = low
        dsrc[2:3] = squares
        return ratio(squares, low)

    def advance(alpha):
        sol_ref[0] = sol_ref[0] + alpha * v[...]
        res_ref[0] = res_ref[0] - alpha * image[...]

    begin_gather(rbuf, r_send, r_sem)
    for copy in loads_in[1:]:
        copy.wait()
    sp = jnp.broadcast_to(spring_row[...], (LOADS, ATT)).T
    spr[...] = sp
    main[...] = jnp.broadcast_to(diag_row[...], (LOADS, ROWS)).T
    main[:ATT] = main[:ATT] + sp
    sol_ref[0] = jnp.zeros((ROWS, LOADS), jnp.float32)
    dsrc[...] = jnp.zeros(dsrc.shape, jnp.float32)

    def first(idx):
        qold[idx] = pre_dot(idx)

    first(d)
    for event in range(COLUMN):
        first(take(rbuf, r_send, r_sem, event, COLUMN + 1 + event))
    for core in range(2):
        @pl.when(c == core)
        def _():
            for k in range(PARTS):
                at, to = k * ATT + core * HALF, k * HALF
                hubblk[:, to:to + HALF] = hubraw[:, at:at + HALF]
    total = qold[zl * NY]
    for k in range(1, NY):
        total = total + qold[zl * NY + k]
    vec[...] = total
    for event in range(NY):
        idx = take_one_across(event)
        product = pre_dot(idx)
        qold[idx] = product
        vec[...] += product
    v[...] = vec[...]
    arrived(rbuf.at[pl.ds(0, BLOCKS)], r_send)
    apply_operator(0, vec, None, None)
    image[...] = acc[...]

    def step(it, carry):
        turn = it % 2
        trial = local_dots()
        rbuf[d] = (res_ref[0] - trial * image[...]).astype(jnp.bfloat16)
        begin_gather(rbuf, r_send, r_sem)
        dots_begin()
        qnew[d] = pre_dot(d)
        for event in range(COLUMN):
            idx = take(rbuf, r_send, r_sem, event, COLUMN + 1 + event)
            qnew[idx] = pre_dot(idx)
            if event == 4:
                dots_pair()
        dots_plane(turn)
        inverse[...] = 1.0 / ratio(dof_dots[:, 2, :], dof_dots[:, 1, :])

        def slope(idx, product):
            diff = (product - qold[idx]) * inverse[pl.ds(idx, 1)]
            qnew[idx] = diff
            return diff

        total = jnp.zeros((ROWS, LOADS), jnp.float32)
        for k in range(NY):
            total = total + slope(zl * NY + k, qnew[zl * NY + k])
        slopes[...] = total
        for event in range(NY):
            idx = take_one_across(event)
            slopes[...] += slope(idx, pre_dot(idx))
        arrived(rbuf.at[pl.ds(0, BLOCKS)], r_send)

        def settle():
            alpha = dots_end(turn)
            vec[...] = v[...] + alpha * slopes[...]
            return alpha

        def late(alpha):
            advance(alpha)
            v[...] = vec[...]
            for k in range(PARTS):
                qold[k] = qold[k] + alpha * qnew[k]

        apply_operator((it + 1) % 2, slopes, settle, late)
        image[...] = acc[...]
        return carry

    lax.fori_loop(0, ITERS - 1, step, 0)
    last = (ITERS - 1) % 2
    local_dots()
    dots_begin()
    dots_pair()
    dots_plane(last)
    alpha = dots_end(last)
    v[...] = alpha * v[...]
    image[...] = alpha * image[...]


def body(rhs, diagonal, coupling, springs, precond, hub_inverse):
    vm = pl.BlockSpec(memory_space=pltpu.VMEM)
    hbm = pl.BlockSpec(memory_space=pltpu.HBM)
    f32, bf16 = jnp.float32, jnp.bfloat16
    dma = pltpu.SemaphoreType.DMA
    mem = pltpu.VMEM
    total, res, v, image = pl.pallas_call(
        kernel,
        out_shape=(
            jax.ShapeDtypeStruct((1, ROWS, LOADS), f32),
            jax.ShapeDtypeStruct((1, ROWS, LOADS), f32),
            jax.ShapeDtypeStruct((ROWS, LOADS), f32),
            jax.ShapeDtypeStruct((ROWS, LOADS), f32),
        ),
        in_specs=[hbm] * 6,
        out_specs=(vm,) * 4,
        scratch_shapes=[
            mem((1, ROWS), f32),
            mem((1, ATT), f32),
            mem((ROWS, PARTS * ROWS), bf16),
            mem((ROWS, PARTS * FACE), bf16),
            mem((ATT, PARTS * ATT), bf16),
            mem((ATT, PARTS * HALF), bf16),
            mem((PARTS, ROWS, LOADS), bf16),
            mem((2, PARTS, FACE, LOADS), bf16),
            mem((PARTS, HALF, LOADS), bf16),
            mem((PARTS, ROWS, LOADS), f32),
            mem((PARTS, ROWS, LOADS), f32),
            mem((FACE, LOADS), bf16),
            mem((ROWS, LOADS), f32),
            mem((ROWS, LOADS), f32),
            mem((PARTS, LOADS), f32),
            mem((ROWS, LOADS), f32),
            mem((ROWS, LOADS), f32),
            mem((ATT, LOADS), f32),
            mem((ATT, LOADS), f32),
            mem((HALF, LOADS), f32),
            mem((ROWS, LOADS), f32),
            mem((ATT, LOADS), f32),
            mem((HALF, LOADS), f32),
            mem((HALF, LOADS), f32),
            mem((HALF, LOADS), f32),
            mem((2, NX, HALF, LOADS), f32),
            mem((HALF, LOADS), f32),
            mem((2, NZH, HALF, LOADS), f32),
            mem((8, LOADS), f32),
            mem((PARTS, 8, LOADS), f32),
            mem((8, LOADS), f32),
            mem((8, LOADS), f32),
            mem((2, NZH * NX, 8, LOADS), f32),
            dma((6,)),
            dma, dma((BLOCKS,)),
            dma, dma((COLUMN + 1,)),
            dma, dma((2, 2)),
            dma, dma,
            dma, dma((2,)),
            dma, dma((2,)),
            dma, dma((COLUMN + 1,)),
            dma, dma,
            dma, dma,
            dma, dma,
            dma, dma((2,)),
        ],
        compiler_params=pltpu.CompilerParams(
            collective_id=0, has_side_effects=True, vmem_limit_bytes=61 * 1024 * 1024
        ),
    )(rhs, diagonal, springs, coupling, precond, hub_inverse)
    return total + v, res - image


def solution(mesh):
    placed = (
        P("sector", "dof", None),
        P("sector", "dof"),
        P("sector", "dof", None),
        P("sector", "dof"),
        P("dof", None),
        P("dof", None),
    )
    return jax.shard_map(
        body,
        mesh=mesh,
        in_specs=placed,
        out_specs=(P("sector", "dof", None), P("sector", "dof", None)),
        check_vma=False,
    )
```

```python
import jax
import jax.numpy as jnp
from jax import lax
from jax.experimental import pallas as pl
from jax.experimental.pallas import tpu as pltpu
from jax.sharding import PartitionSpec as P

ITERS = 3
NX, NY, NZL, NZH = 4, 8, 2, 4
PARTS = NY * NZL
QUARTER = 64
ROWS = 4 * QUARTER
FACE = 2 * QUARTER
ATT = 3 * QUARTER
HALF = ATT // 2
LOADS = 128
MESH = pl.DeviceIdType.MESH

NEAR = (-2, 2, -1, 1, -3, 3, -4)
COLUMN = len(NEAR)
BLOCKS = 2 * COLUMN + 1


def kernel(
    rhs_hbm, diag_hbm, spring_hbm, couple_hbm, pre_hbm, hub_hbm, sol_ref, res_ref, v, image,
    diag_row, spring_row, pre, coup, hubraw, hubblk, rbuf, fbuf, lbuf, qold, qnew, stage,
    vec, slopes, inverse, acc, cacc, hacc, hrecv, load, main, spr, csend, crecv, xsend, xrecv, zsend, zrecv, dsrc, dof_dots, pair_src, pair_dots, all_dots,
    load_sem, r_send, r_sem, f_send, f_sem, n_send, n_sem, c_send, c_sem, x_send, x_sem,
    z_send, z_sem, y_send, y_sem, h_send, h_sem, d_send, d_sem, p_send, p_sem, a_send, a_sem,
):
    s = lax.axis_index("sector")
    d = lax.axis_index("dof")
    zh, x, c = s // (2 * NX), (s // 2) % NX, s % 2
    zl, y = d // NY, d % NY
    plane = zh * NX + x
    nsec = NZH * NX * 2

    def sector_of(zh, x, c):
        return (zh * NX + x) * 2 + c

    def dof_at(column, offset):
        col = zl if column == 0 else 1 - zl
        return col * NY + (y + offset + NY) % NY

    zh_peer = [(sector_of((zh + k) % NZH, x, c), d) for k in range(NZH)]
    x_peer = [(sector_of(zh, (x + j) % NX, c), d) for j in range(NX)]
    dof_peer = [(s, (d + j) % PARTS) for j in range(PARTS)]
    plane_at = [(plane + j) % (NZH * NX) for j in range(NZH * NX)]
    plane_peer = [(m * 2 + c, d) for m in plane_at]
    partner = (s, dof_at(1, 0))
    sibling = (sector_of(zh, x, 1 - c), d)
    next_sec = ((s + 1) % nsec, d)
    prev_sec = ((s + nsec - 1) % nsec, d)

    def send(src, dst, ssem, rsem, dev):
        pltpu.make_async_remote_copy(
            src_ref=src, dst_ref=dst, send_sem=ssem, recv_sem=rsem,
            device_id=dev, device_id_type=MESH,
        ).start()

    def arrived(ref, sem):
        pltpu.make_async_copy(ref, ref, sem).wait()

    loads_in = [
        pltpu.make_async_copy(rhs_hbm, res_ref, load_sem.at[0]),
        pltpu.make_async_copy(pre_hbm, pre, load_sem.at[1]),
        pltpu.make_async_copy(diag_hbm, diag_row, load_sem.at[2]),
        pltpu.make_async_copy(spring_hbm, spring_row, load_sem.at[3]),
        pltpu.make_async_copy(hub_hbm, hubraw, load_sem.at[4]),
        pltpu.make_async_copy(couple_hbm.at[0], coup, load_sem.at[5]),
    ]
    barrier = pltpu.get_barrier_semaphore()
    greet = plane_peer[1:] + dof_peer[1:] + [sibling, next_sec, prev_sec]
    for dev in greet:
        pl.semaphore_signal(barrier, inc=1, device_id=dev, device_id_type=MESH)
    for copy in loads_in:
        copy.start()
    loads_in[0].wait()
    rbuf[d] = res_ref[0].astype(jnp.bfloat16)
    pl.semaphore_wait(barrier, len(greet))

    def begin_gather(buf, ssem, rsem):
        for k, offset in enumerate(NEAR[:-1]):
            send(buf.at[d], buf.at[d], ssem, rsem.at[k], (s, dof_at(0, -offset)))
        send(buf.at[d], buf.at[d], ssem, rsem.at[COLUMN], partner)

    def take(buf, ssem, rsem, event, onward=COLUMN):
        idx = dof_at(0, NEAR[event])
        arrived(buf.at[idx], rsem.at[event])
        if event == 0:
            send(buf.at[idx], buf.at[idx], ssem, rsem.at[COLUMN - 1], (s, dof_at(0, 2)))
        send(buf.at[idx], buf.at[idx], ssem, rsem.at[onward], partner)
        return idx

    def take_one_across(event):
        idx = dof_at(1, ((0,) + NEAR)[event])
        arrived(rbuf.at[idx], r_sem.at[COLUMN + event])
        return idx

    across_first = (1 - zl) * NY

    def take_across(buf, rsem):
        arrived(buf.at[pl.ds(across_first, NY)], rsem.at[COLUMN])

    def pre_dot(idx):
        off = pl.multiple_of(idx * ROWS, ROWS)
        return jnp.dot(pre[:, pl.ds(off, ROWS)], rbuf[idx], preferred_element_type=jnp.float32)

    def couple_dot(faces, first, count):
        off = pl.multiple_of(first * FACE, FACE)
        rows = faces[pl.ds(first, count)].reshape(count * FACE, LOADS)
        return jnp.dot(coup[:, pl.ds(off, count * FACE)], rows, preferred_element_type=jnp.float32)

    def hub_dot(first):
        off = pl.multiple_of(first * HALF, NY * HALF)
        rows = lbuf[pl.ds(first, NY)].reshape(NY * HALF, LOADS)
        return jnp.dot(hubblk[:, pl.ds(off, NY * HALF)], rows, preferred_element_type=jnp.float32)

    def ratio(squares, low):
        return jnp.clip(jnp.sqrt(squares / jnp.maximum(low, 1e-30)), 1e-12, 1e12)

    def apply_operator(turn, source, settle, late):
        faces = fbuf.at[turn]
        right, left = pl.ds(QUARTER, QUARTER), pl.ds(0, QUARTER)

        def send_faces():
            stage[...] = vec[:FACE].astype(jnp.bfloat16)
            send(stage.at[right], faces.at[d, left], n_send, n_sem.at[turn, 0], next_sec)
            send(stage.at[left], faces.at[d, right], n_send, n_sem.at[turn, 1], prev_sec)

        def gather_faces():
            arrived(faces.at[d, left], n_sem.at[turn, 0])
            arrived(faces.at[d, right], n_sem.at[turn, 1])
            begin_gather(faces, f_send, f_sem)

        def face(event):
            cacc[...] += couple_dot(faces, take(faces, f_send, f_sem, event), 1)

        other = pl.multiple_of((1 - c) * HALF, 8)
        mine = pl.multiple_of(c * HALF, 8)
        csend[...] = spr[pl.ds(other, HALF)] * source[pl.ds(other, HALF)]
        send(csend, crecv, c_send, c_sem, sibling)
        if settle is None:
            send_faces()
        part = spr[pl.ds(mine, HALF)] * source[pl.ds(mine, HALF)]
        arrived(crecv, c_sem)
        part = part + crecv[...]
        xsend[...] = part
        for j in range(1, NX):
            send(xsend, xrecv.at[turn, j], x_send, x_sem.at[turn], x_peer[j])
        if settle is None:
            gather_faces()
        else:
            alpha = settle()
            send_faces()
            late(alpha)
        arrived(xrecv.at[turn, pl.ds(1, NX - 1)], x_sem.at[turn])
        part = part + xrecv[turn, 1] + xrecv[turn, 2] + xrecv[turn, 3]
        zsend[...] = part
        for k in range(1, NZH):
            send(zsend, zrecv.at[turn, k], z_send, z_sem.at[turn], zh_peer[k])
        ahead = 0
        if settle is None:
            cacc[...] = couple_dot(faces, d, 1)
            for event in range(COLUMN):
                face(event)
            ahead = COLUMN
        else:
            gather_faces()
            cacc[...] = couple_dot(faces, d, 1)
        arrived(zrecv.at[turn, pl.ds(1, NZH - 1)], z_sem.at[turn])
        part = part + zrecv[turn, 1] + zrecv[turn, 2] + zrecv[turn, 3]
        if settle is not None:
            part = load[...] + alpha * part
        load[...] = part
        lbuf[d] = part.astype(jnp.bfloat16)
        begin_gather(lbuf, y_send, y_sem)
        for event in range(ahead, 4):
            face(event)
        for event in range(COLUMN):
            take(lbuf, y_send, y_sem, event)
            if max(ahead, 4) <= event + 4 < COLUMN:
                face(event + 4)
        take_across(faces, f_sem)
        acc[...] = main[...] * vec[...] + cacc[...] + couple_dot(faces, across_first, NY)
        arrived(csend, c_send)
        arrived(stage, n_send)
        arrived(xrecv.at[turn, pl.ds(0, NX - 1)], x_send)
        arrived(faces.at[pl.ds(0, BLOCKS)], f_send)
        arrived(zrecv.at[turn, pl.ds(0, NZH - 1)], z_send)
        hacc[...] = hub_dot(zl * NY)
        take_across(lbuf, y_sem)
        hacc[...] += hub_dot(across_first)
        send(hacc, hrecv, h_send, h_sem, sibling)
        arrived(hrecv, h_sem)
        acc[:ATT] = acc[:ATT] - spr[...] * (hacc[...] + hrecv[...])
        arrived(hacc, h_send)
        arrived(lbuf.at[pl.ds(0, BLOCKS)], y_send)

    def column_sum(a):
        return jnp.sum(a, axis=0, keepdims=True)

    def dots_begin():
        dsrc[0:1] = column_sum(image[...] * res_ref[0])
        for j in range(1, PARTS):
            send(dsrc, dof_dots.at[d], d_send, d_sem, dof_peer[j])
        dof_dots[d] = dsrc[...]

    def dots_pair():
        arrived(dof_dots.at[pl.ds(0, PARTS - 1)], d_sem)
        pair_src[...] = jnp.sum(dof_dots[...], axis=0)
        send(pair_src, pair_dots, p_send, p_sem, sibling)

    def dots_plane(turn):
        arrived(pair_dots, p_sem)
        dots = all_dots.at[turn]
        dots[plane] = pair_src[...] + pair_dots[...]
        for j in range(1, NZH * NX):
            send(dots.at[plane], dots.at[plane], a_send, a_sem.at[turn], plane_peer[j])

    def dots_end(turn):
        arrived(all_dots.at[turn, pl.ds(0, NZH * NX - 1)], a_sem.at[turn])
        total = jnp.sum(all_dots[turn], axis=0)
        arrived(dof_dots.at[pl.ds(0, PARTS - 1)], d_send)
        arrived(pair_src, p_send)
        arrived(all_dots.at[turn, pl.ds(0, NZH * NX - 1)], a_send)
        return total[0:1] / (total[1:2] + 1e-06)

    def local_dots():
        im, res = image[...], res_ref[0]
        low, squares = column_sum(im * im), column_sum(res * res)
        dsrc[1:2] = low
        dsrc[2:3] = squares
        return ratio(squares, low)

    def advance(alpha):
        sol_ref[0] = sol_ref[0] + alpha * v[...]
        res_ref[0] = res_ref[0] - alpha * image[...]

    begin_gather(rbuf, r_send, r_sem)
    for copy in loads_in[1:]:
        copy.wait()
    sp = jnp.broadcast_to(spring_row[...], (LOADS, ATT)).T
    spr[...] = sp
    main[...] = jnp.broadcast_to(diag_row[...], (LOADS, ROWS)).T
    main[:ATT] = main[:ATT] + sp
    sol_ref[0] = jnp.zeros((ROWS, LOADS), jnp.float32)
    dsrc[...] = jnp.zeros(dsrc.shape, jnp.float32)

    def first(idx):
        qold[idx] = pre_dot(idx)

    first(d)
    for event in range(COLUMN):
        first(take(rbuf, r_send, r_sem, event, COLUMN + 1 + event))
    for core in range(2):
        @pl.when(c == core)
        def _():
            for k in range(PARTS):
                at, to = k * ATT + core * HALF, k * HALF
                hubblk[:, to:to + HALF] = hubraw[:, at:at + HALF]
    total = qold[zl * NY]
    for k in range(1, NY):
        total = total + qold[zl * NY + k]
    vec[...] = total
    for event in range(NY):
        idx = take_one_across(event)
        product = pre_dot(idx)
        qold[idx] = product
        vec[...] += product
    v[...] = vec[...]
    arrived(rbuf.at[pl.ds(0, BLOCKS)], r_send)
    apply_operator(0, vec, None, None)
    image[...] = acc[...]

    def step(it, carry):
        turn = it % 2
        trial = local_dots()
        rbuf[d] = (res_ref[0] - trial * image[...]).astype(jnp.bfloat16)
        begin_gather(rbuf, r_send, r_sem)
        dots_begin()
        qnew[d] = pre_dot(d)
        for event in range(COLUMN):
            idx = take(rbuf, r_send, r_sem, event, COLUMN + 1 + event)
            qnew[idx] = pre_dot(idx)
            if event == 3:
                dots_pair()
            if event == 5:
                dots_plane(turn)
        inverse[...] = 1.0 / ratio(dof_dots[:, 2, :], dof_dots[:, 1, :])

        def slope(idx, product):
            diff = (product - qold[idx]) * inverse[pl.ds(idx, 1)]
            qnew[idx] = diff
            return diff

        total = jnp.zeros((ROWS, LOADS), jnp.float32)
        for k in range(NY):
            total = total + slope(zl * NY + k, qnew[zl * NY + k])
        slopes[...] = total
        for event in range(NY):
            idx = take_one_across(event)
            slopes[...] += slope(idx, pre_dot(idx))
        arrived(rbuf.at[pl.ds(0, BLOCKS)], r_send)

        def settle():
            alpha = dots_end(turn)
            vec[...] = v[...] + alpha * slopes[...]
            return alpha

        def late(alpha):
            advance(alpha)
            v[...] = vec[...]
            for k in range(PARTS):
                qold[k] = qold[k] + alpha * qnew[k]

        apply_operator((it + 1) % 2, slopes, settle, late)
        image[...] = acc[...]
        return carry

    lax.fori_loop(0, ITERS - 1, step, 0)
    last = (ITERS - 1) % 2
    local_dots()
    dots_begin()
    dots_pair()
    dots_plane(last)
    alpha = dots_end(last)
    v[...] = alpha * v[...]
    image[...] = alpha * image[...]


def body(rhs, diagonal, coupling, springs, precond, hub_inverse):
    vm = pl.BlockSpec(memory_space=pltpu.VMEM)
    hbm = pl.BlockSpec(memory_space=pltpu.HBM)
    f32, bf16 = jnp.float32, jnp.bfloat16
    dma = pltpu.SemaphoreType.DMA
    mem = pltpu.VMEM
    total, res, v, image = pl.pallas_call(
        kernel,
        out_shape=(
            jax.ShapeDtypeStruct((1, ROWS, LOADS), f32),
            jax.ShapeDtypeStruct((1, ROWS, LOADS), f32),
            jax.ShapeDtypeStruct((ROWS, LOADS), f32),
            jax.ShapeDtypeStruct((ROWS, LOADS), f32),
        ),
        in_specs=[hbm] * 6,
        out_specs=(vm,) * 4,
        scratch_shapes=[
            mem((1, ROWS), f32),
            mem((1, ATT), f32),
            mem((ROWS, PARTS * ROWS), bf16),
            mem((ROWS, PARTS * FACE), bf16),
            mem((ATT, PARTS * ATT), bf16),
            mem((ATT, PARTS * HALF), bf16),
            mem((PARTS, ROWS, LOADS), bf16),
            mem((2, PARTS, FACE, LOADS), bf16),
            mem((PARTS, HALF, LOADS), bf16),
            mem((PARTS, ROWS, LOADS), f32),
            mem((PARTS, ROWS, LOADS), f32),
            mem((FACE, LOADS), bf16),
            mem((ROWS, LOADS), f32),
            mem((ROWS, LOADS), f32),
            mem((PARTS, LOADS), f32),
            mem((ROWS, LOADS), f32),
            mem((ROWS, LOADS), f32),
            mem((ATT, LOADS), f32),
            mem((ATT, LOADS), f32),
            mem((HALF, LOADS), f32),
            mem((ROWS, LOADS), f32),
            mem((ATT, LOADS), f32),
            mem((HALF, LOADS), f32),
            mem((HALF, LOADS), f32),
            mem((HALF, LOADS), f32),
            mem((2, NX, HALF, LOADS), f32),
            mem((HALF, LOADS), f32),
            mem((2, NZH, HALF, LOADS), f32),
            mem((8, LOADS), f32),
            mem((PARTS, 8, LOADS), f32),
            mem((8, LOADS), f32),
            mem((8, LOADS), f32),
            mem((2, NZH * NX, 8, LOADS), f32),
            dma((6,)),
            dma, dma((BLOCKS,)),
            dma, dma((COLUMN + 1,)),
            dma, dma((2, 2)),
            dma, dma,
            dma, dma((2,)),
            dma, dma((2,)),
            dma, dma((COLUMN + 1,)),
            dma, dma,
            dma, dma,
            dma, dma,
            dma, dma((2,)),
        ],
        compiler_params=pltpu.CompilerParams(
            collective_id=0, has_side_effects=True, vmem_limit_bytes=61 * 1024 * 1024
        ),
    )(rhs, diagonal, springs, coupling, precond, hub_inverse)
    return total + v, res - image


def solution(mesh):
    placed = (
        P("sector", "dof", None),
        P("sector", "dof"),
        P("sector", "dof", None),
        P("sector", "dof"),
        P("dof", None),
        P("dof", None),
    )
    return jax.shard_map(
        body,
        mesh=mesh,
        in_specs=placed,
        out_specs=(P("sector", "dof", None), P("sector", "dof", None)),
        check_vma=False,
    )
```

```python
import jax
import jax.numpy as jnp
from jax import lax
from jax.experimental import pallas as pl
from jax.experimental.pallas import tpu as pltpu
from jax.sharding import PartitionSpec as P

ITERS = 3
NX, NY, NZL, NZH = 4, 8, 2, 4
PARTS = NY * NZL
QUARTER = 64
ROWS = 4 * QUARTER
FACE = 2 * QUARTER
ATT = 3 * QUARTER
HALF = ATT // 2
LOADS = 128
MESH = pl.DeviceIdType.MESH

NEAR = (-2, 2, -1, 1, -3, 3, -4)
COLUMN = len(NEAR)
BLOCKS = 2 * COLUMN + 1


def kernel(
    rhs_hbm, diag_hbm, spring_hbm, couple_hbm, pre_hbm, hub_hbm, sol_ref, res_ref, v, image,
    diag_row, spring_row, pre, coup, hubraw, hubblk, rbuf, fbuf, lbuf, qold, qnew, stage,
    vec, slopes, inverse, acc, cacc, hacc, hrecv, load, main, spr, csend, crecv, xsend, xrecv, zsend, zrecv, dsrc, dof_dots, pair_src, pair_dots, all_dots,
    load_sem, r_send, r_sem, f_send, f_sem, n_send, n_sem, c_send, c_sem, x_send, x_sem,
    z_send, z_sem, y_send, y_sem, h_send, h_sem, d_send, d_sem, p_send, p_sem, a_send, a_sem,
):
    s = lax.axis_index("sector")
    d = lax.axis_index("dof")
    zh, x, c = s // (2 * NX), (s // 2) % NX, s % 2
    zl, y = d // NY, d % NY
    plane = zh * NX + x
    nsec = NZH * NX * 2

    def sector_of(zh, x, c):
        return (zh * NX + x) * 2 + c

    def dof_at(column, offset):
        col = zl if column == 0 else 1 - zl
        return col * NY + (y + offset + NY) % NY

    zh_peer = [(sector_of((zh + k) % NZH, x, c), d) for k in range(NZH)]
    x_peer = [(sector_of(zh, (x + j) % NX, c), d) for j in range(NX)]
    dof_peer = [(s, (d + j) % PARTS) for j in range(PARTS)]
    plane_at = [(plane + j) % (NZH * NX) for j in range(NZH * NX)]
    plane_peer = [(m * 2 + c, d) for m in plane_at]
    partner = (s, dof_at(1, 0))
    sibling = (sector_of(zh, x, 1 - c), d)
    next_sec = ((s + 1) % nsec, d)
    prev_sec = ((s + nsec - 1) % nsec, d)

    def send(src, dst, ssem, rsem, dev):
        pltpu.make_async_remote_copy(
            src_ref=src, dst_ref=dst, send_sem=ssem, recv_sem=rsem,
            device_id=dev, device_id_type=MESH,
        ).start()

    def arrived(ref, sem):
        pltpu.make_async_copy(ref, ref, sem).wait()

    loads_in = [
        pltpu.make_async_copy(rhs_hbm, res_ref, load_sem.at[0]),
        pltpu.make_async_copy(pre_hbm, pre, load_sem.at[1]),
        pltpu.make_async_copy(diag_hbm, diag_row, load_sem.at[2]),
        pltpu.make_async_copy(spring_hbm, spring_row, load_sem.at[3]),
        pltpu.make_async_copy(hub_hbm, hubraw, load_sem.at[4]),
        pltpu.make_async_copy(couple_hbm.at[0], coup, load_sem.at[5]),
    ]
    barrier = pltpu.get_barrier_semaphore()
    greet = plane_peer[1:] + dof_peer[1:] + [sibling, next_sec, prev_sec]
    for dev in greet:
        pl.semaphore_signal(barrier, inc=1, device_id=dev, device_id_type=MESH)
    for copy in loads_in:
        copy.start()
    loads_in[0].wait()
    rbuf[d] = res_ref[0].astype(jnp.bfloat16)
    pl.semaphore_wait(barrier, len(greet))

    def begin_gather(buf, ssem, rsem):
        for k, offset in enumerate(NEAR[:-1]):
            send(buf.at[d], buf.at[d], ssem, rsem.at[k], (s, dof_at(0, -offset)))
        send(buf.at[d], buf.at[d], ssem, rsem.at[COLUMN], partner)

    def take(buf, ssem, rsem, event, onward=COLUMN):
        idx = dof_at(0, NEAR[event])
        arrived(buf.at[idx], rsem.at[event])
        if event == 0:
            send(buf.at[idx], buf.at[idx], ssem, rsem.at[COLUMN - 1], (s, dof_at(0, 2)))
        send(buf.at[idx], buf.at[idx], ssem, rsem.at[onward], partner)
        return idx

    def take_one_across(event):
        idx = dof_at(1, ((0,) + NEAR)[event])
        arrived(rbuf.at[idx], r_sem.at[COLUMN + event])
        return idx

    across_first = (1 - zl) * NY

    def take_across(buf, rsem):
        arrived(buf.at[pl.ds(across_first, NY)], rsem.at[COLUMN])

    def pre_dot(idx):
        off = pl.multiple_of(idx * ROWS, ROWS)
        return jnp.dot(pre[:, pl.ds(off, ROWS)], rbuf[idx], preferred_element_type=jnp.float32)

    def couple_dot(faces, first, count):
        off = pl.multiple_of(first * FACE, FACE)
        rows = faces[pl.ds(first, count)].reshape(count * FACE, LOADS)
        return jnp.dot(coup[:, pl.ds(off, count * FACE)], rows, preferred_element_type=jnp.float32)

    def hub_dot(first):
        off = pl.multiple_of(first * HALF, NY * HALF)
        rows = lbuf[pl.ds(first, NY)].reshape(NY * HALF, LOADS)
        return jnp.dot(hubblk[:, pl.ds(off, NY * HALF)], rows, preferred_element_type=jnp.float32)

    def ratio(squares, low):
        return jnp.clip(jnp.sqrt(squares / jnp.maximum(low, 1e-30)), 1e-12, 1e12)

    def apply_operator(turn, source, settle, late):
        faces = fbuf.at[turn]
        right, left = pl.ds(QUARTER, QUARTER), pl.ds(0, QUARTER)

        def send_faces():
            stage[...] = vec[:FACE].astype(jnp.bfloat16)
            send(stage.at[right], faces.at[d, left], n_send, n_sem.at[turn, 0], next_sec)
            send(stage.at[left], faces.at[d, right], n_send, n_sem.at[turn, 1], prev_sec)

        def gather_faces():
            arrived(faces.at[d, left], n_sem.at[turn, 0])
            arrived(faces.at[d, right], n_sem.at[turn, 1])
            begin_gather(faces, f_send, f_sem)

        def face(event):
            cacc[...] += couple_dot(faces, take(faces, f_send, f_sem, event), 1)

        other = pl.multiple_of((1 - c) * HALF, 8)
        mine = pl.multiple_of(c * HALF, 8)
        csend[...] = spr[pl.ds(other, HALF)] * source[pl.ds(other, HALF)]
        send(csend, crecv, c_send, c_sem, sibling)
        if settle is None:
            send_faces()
        part = spr[pl.ds(mine, HALF)] * source[pl.ds(mine, HALF)]
        arrived(crecv, c_sem)
        part = part + crecv[...]
        xsend[...] = part
        for j in range(1, NX):
            send(xsend, xrecv.at[turn, j], x_send, x_sem.at[turn], x_peer[j])
        if settle is None:
            gather_faces()
        else:
            alpha = settle()
            send_faces()
            late(alpha)
        arrived(xrecv.at[turn, pl.ds(1, NX - 1)], x_sem.at[turn])
        part = part + xrecv[turn, 1] + xrecv[turn, 2] + xrecv[turn, 3]
        zsend[...] = part
        for k in range(1, NZH):
            send(zsend, zrecv.at[turn, k], z_send, z_sem.at[turn], zh_peer[k])
        ahead = 0
        if settle is None:
            cacc[...] = couple_dot(faces, d, 1)
            for event in range(COLUMN):
                face(event)
            ahead = COLUMN
        else:
            gather_faces()
            cacc[...] = couple_dot(faces, d, 1)
        arrived(zrecv.at[turn, pl.ds(1, NZH - 1)], z_sem.at[turn])
        part = part + zrecv[turn, 1] + zrecv[turn, 2] + zrecv[turn, 3]
        if settle is not None:
            part = load[...] + alpha * part
        load[...] = part
        lbuf[d] = part.astype(jnp.bfloat16)
        begin_gather(lbuf, y_send, y_sem)
        for event in range(ahead, 4):
            face(event)
        for event in range(COLUMN):
            take(lbuf, y_send, y_sem, event)
            if max(ahead, 4) <= event + 4 < COLUMN:
                face(event + 4)
        take_across(faces, f_sem)
        acc[...] = main[...] * vec[...] + cacc[...] + couple_dot(faces, across_first, NY)
        arrived(csend, c_send)
        arrived(stage, n_send)
        arrived(xrecv.at[turn, pl.ds(0, NX - 1)], x_send)
        arrived(faces.at[pl.ds(0, BLOCKS)], f_send)
        arrived(zrecv.at[turn, pl.ds(0, NZH - 1)], z_send)
        hacc[...] = hub_dot(zl * NY)
        take_across(lbuf, y_sem)
        hacc[...] += hub_dot(across_first)
        send(hacc, hrecv, h_send, h_sem, sibling)
        arrived(hrecv, h_sem)
        acc[:ATT] = acc[:ATT] - spr[...] * (hacc[...] + hrecv[...])
        arrived(hacc, h_send)
        arrived(lbuf.at[pl.ds(0, BLOCKS)], y_send)

    def column_sum(a):
        return jnp.sum(a, axis=0, keepdims=True)

    def dots_begin():
        dsrc[0:1] = column_sum(image[...] * res_ref[0])
        for j in range(1, PARTS):
            send(dsrc, dof_dots.at[d], d_send, d_sem, dof_peer[j])
        dof_dots[d] = dsrc[...]

    def dots_pair():
        arrived(dof_dots.at[pl.ds(0, PARTS - 1)], d_sem)
        pair_src[...] = jnp.sum(dof_dots[...], axis=0)
        send(pair_src, pair_dots, p_send, p_sem, sibling)

    def dots_plane(turn):
        arrived(pair_dots, p_sem)
        dots = all_dots.at[turn]
        dots[plane] = pair_src[...] + pair_dots[...]
        for j in range(1, NZH * NX):
            send(dots.at[plane], dots.at[plane], a_send, a_sem.at[turn], plane_peer[j])

    def dots_end(turn):
        arrived(all_dots.at[turn, pl.ds(0, NZH * NX - 1)], a_sem.at[turn])
        total = jnp.sum(all_dots[turn], axis=0)
        arrived(dof_dots.at[pl.ds(0, PARTS - 1)], d_send)
        arrived(pair_src, p_send)
        arrived(all_dots.at[turn, pl.ds(0, NZH * NX - 1)], a_send)
        return total[0:1] / (total[1:2] + 1e-06)

    def local_dots():
        im, res = image[...], res_ref[0]
        low, squares = column_sum(im * im), column_sum(res * res)
        dsrc[1:2] = low
        dsrc[2:3] = squares
        return ratio(squares, low)

    def advance(alpha):
        sol_ref[0] = sol_ref[0] + alpha * v[...]
        res_ref[0] = res_ref[0] - alpha * image[...]

    begin_gather(rbuf, r_send, r_sem)
    for copy in loads_in[1:]:
        copy.wait()
    sp = jnp.broadcast_to(spring_row[...], (LOADS, ATT)).T
    spr[...] = sp
    main[...] = jnp.broadcast_to(diag_row[...], (LOADS, ROWS)).T
    main[:ATT] = main[:ATT] + sp
    sol_ref[0] = jnp.zeros((ROWS, LOADS), jnp.float32)
    dsrc[...] = jnp.zeros(dsrc.shape, jnp.float32)

    def first(idx):
        qold[idx] = pre_dot(idx)

    first(d)
    for event in range(COLUMN):
        first(take(rbuf, r_send, r_sem, event, COLUMN + 1 + event))
    for core in range(2):
        @pl.when(c == core)
        def _():
            for k in range(PARTS):
                at, to = k * ATT + core * HALF, k * HALF
                hubblk[:, to:to + HALF] = hubraw[:, at:at + HALF]
    total = qold[zl * NY]
    for k in range(1, NY):
        total = total + qold[zl * NY + k]
    vec[...] = total
    for event in range(NY):
        idx = take_one_across(event)
        product = pre_dot(idx)
        qold[idx] = product
        vec[...] += product
    v[...] = vec[...]
    arrived(rbuf.at[pl.ds(0, BLOCKS)], r_send)
    apply_operator(0, vec, None, None)
    image[...] = acc[...]

    def step(it, carry):
        turn = it % 2
        trial = local_dots()
        rbuf[d] = (res_ref[0] - trial * image[...]).astype(jnp.bfloat16)
        begin_gather(rbuf, r_send, r_sem)
        dots_begin()
        qnew[d] = pre_dot(d)
        for event in range(COLUMN):
            idx = take(rbuf, r_send, r_sem, event, COLUMN + 1 + event)
            qnew[idx] = pre_dot(idx)
            if event == 4:
                dots_pair()
        dots_plane(turn)
        inverse[...] = 1.0 / ratio(dof_dots[:, 2, :], dof_dots[:, 1, :])

        def slope(idx, product):
            diff = (product - qold[idx]) * inverse[pl.ds(idx, 1)]
            qnew[idx] = diff
            return diff

        total = jnp.zeros((ROWS, LOADS), jnp.float32)
        for k in range(NY):
            total = total + slope(zl * NY + k, qnew[zl * NY + k])
        slopes[...] = total
        for event in range(NY):
            idx = take_one_across(event)
            slopes[...] += slope(idx, pre_dot(idx))
        arrived(rbuf.at[pl.ds(0, BLOCKS)], r_send)

        def settle():
            alpha = dots_end(turn)
            vec[...] = v[...] + alpha * slopes[...]
            return alpha

        def late(alpha):
            advance(alpha)
            v[...] = vec[...]
            for k in range(PARTS):
                qold[k] = qold[k] + alpha * qnew[k]

        apply_operator((it + 1) % 2, slopes, settle, late)
        image[...] = acc[...]
        return carry

    lax.fori_loop(0, ITERS - 1, step, 0)
    last = (ITERS - 1) % 2
    local_dots()
    dots_begin()
    dots_pair()
    dots_plane(last)
    alpha = dots_end(last)
    v[...] = alpha * v[...]
    image[...] = alpha * image[...]


def body(rhs, diagonal, coupling, springs, precond, hub_inverse):
    vm = pl.BlockSpec(memory_space=pltpu.VMEM)
    hbm = pl.BlockSpec(memory_space=pltpu.HBM)
    f32, bf16 = jnp.float32, jnp.bfloat16
    dma = pltpu.SemaphoreType.DMA
    mem = pltpu.VMEM
    total, res, v, image = pl.pallas_call(
        kernel,
        out_shape=(
            jax.ShapeDtypeStruct((1, ROWS, LOADS), f32),
            jax.ShapeDtypeStruct((1, ROWS, LOADS), f32),
            jax.ShapeDtypeStruct((ROWS, LOADS), f32),
            jax.ShapeDtypeStruct((ROWS, LOADS), f32),
        ),
        in_specs=[hbm] * 6,
        out_specs=(vm,) * 4,
        scratch_shapes=[
            mem((1, ROWS), f32),
            mem((1, ATT), f32),
            mem((ROWS, PARTS * ROWS), bf16),
            mem((ROWS, PARTS * FACE), bf16),
            mem((ATT, PARTS * ATT), bf16),
            mem((ATT, PARTS * HALF), bf16),
            mem((PARTS, ROWS, LOADS), bf16),
            mem((2, PARTS, FACE, LOADS), bf16),
            mem((PARTS, HALF, LOADS), bf16),
            mem((PARTS, ROWS, LOADS), f32),
            mem((PARTS, ROWS, LOADS), f32),
            mem((FACE, LOADS), bf16),
            mem((ROWS, LOADS), f32),
            mem((ROWS, LOADS), f32),
            mem((PARTS, LOADS), f32),
            mem((ROWS, LOADS), f32),
            mem((ROWS, LOADS), f32),
            mem((ATT, LOADS), f32),
            mem((ATT, LOADS), f32),
            mem((HALF, LOADS), f32),
            mem((ROWS, LOADS), f32),
            mem((ATT, LOADS), f32),
            mem((HALF, LOADS), f32),
            mem((HALF, LOADS), f32),
            mem((HALF, LOADS), f32),
            mem((2, NX, HALF, LOADS), f32),
            mem((HALF, LOADS), f32),
            mem((2, NZH, HALF, LOADS), f32),
            mem((8, LOADS), f32),
            mem((PARTS, 8, LOADS), f32),
            mem((8, LOADS), f32),
            mem((8, LOADS), f32),
            mem((2, NZH * NX, 8, LOADS), f32),
            dma((6,)),
            dma, dma((BLOCKS,)),
            dma, dma((COLUMN + 1,)),
            dma, dma((2, 2)),
            dma, dma,
            dma, dma((2,)),
            dma, dma((2,)),
            dma, dma((COLUMN + 1,)),
            dma, dma,
            dma, dma,
            dma, dma,
            dma, dma((2,)),
        ],
        compiler_params=pltpu.CompilerParams(
            collective_id=0, has_side_effects=True, vmem_limit_bytes=61 * 1024 * 1024
        ),
    )(rhs, diagonal, springs, coupling, precond, hub_inverse)
    return total + v, res - image


def solution(mesh):
    placed = (
        P("sector", "dof", None),
        P("sector", "dof"),
        P("sector", "dof", None),
        P("sector", "dof"),
        P("dof", None),
        P("dof", None),
    )
    return jax.shard_map(
        body,
        mesh=mesh,
        in_specs=placed,
        out_specs=(P("sector", "dof", None), P("sector", "dof", None)),
        check_vma=False,
    )
```
